128 devices in a mesh: row: 64 (over z, y_lo, x, core), chan: 2 (over y_hi).
Axes of the slice: x: 4, y: 4 (y_hi: 2, y_lo: 2; y = y_hi * 2 + y_lo), z: 4, core: 2. Of those that a mesh axis runs over, the one named last changes fastest.
Arguments:
- sky_image: float32 [2, 4096, 4096], P('chan', 'row'), may hold values from -6 to 6
- fourier_dual: float32 [2, 2, 4096, 4096], P(None, 'chan', 'row'), may hold values from -6 to 6
- visibilities: float32 [2, 2, 4096, 4096], P(None, 'chan', 'row'), may hold values from -18 to 18
- weights: float32 [2, 4096, 4096], P('chan', 'row'), may hold values from 0.1 to 1
- radius: float32 [2], P('chan'), may hold values from 0.2 to 0.6
- wavelet_dual: float32 [2, 4096, 4096], P(None, ('row', 'chan')), may hold values from -6 to 6
- reweight: float32 [4096, 4096], P(('row', 'chan')), may hold values from 0.3 to 3
Outputs:
- image_new: float32 [2, 4096, 4096], P('chan', 'row')
- fourier_new: float32 [2, 2, 4096, 4096], P(None, 'chan', 'row')
- wavelet_new: float32 [2, 4096, 4096], P(None, ('row', 'chan'))
The draws below stay inside these ranges and needn't reach their ends.
All inputs are finite; a program needn't handle non-finite values.
Results may differ from the reference program's by a relative error of at most 0.000084.
Values sent between devices are 32-bit elements; how exact they have to be, the bound alone decides.
A program may use at most 128 MiB of HBM per device.

```python
import math
import jax
import jax.numpy as jnp
from jax import lax

N = 4096
C = 2


def draw_visibilities(key, part):
    array_shape = (2, C, N, N)
    fraction = jnp.arange(N, dtype=jnp.float32) / (N - 1)
    entries = jax.random.truncated_normal(key, -6.0, 6.0, array_shape, jnp.float32)
    row_scale = 1.0 + 2.0 * fraction
    return entries * row_scale[None, None, :, None]


def block_scale(own_key, extent, cuts, least, largest):
    def one(position, shards_of):
        draws = jax.random.uniform(jax.random.fold_in(jax.random.fold_in(own_key, 6), position), (shards_of,), jnp.float32, least / len(cuts), largest / len(cuts))
        return jnp.repeat(jnp.exp(draws), extent[position] // shards_of).reshape((-1,) + (1,) * (len(extent) - position - 1))

    factor_of = one(*cuts[0])
    for cut in cuts[1:]:
        factor_of = factor_of * one(*cut)
    return factor_of


def scatter_about(key, dims, deviation, reach, shards=(), held_as=jnp.bfloat16):
    values = deviation * jax.random.normal(key, dims, jnp.float32)
    if shards:
        values = values * block_scale(key, dims, shards, -0.22, 0.18)
    return jnp.clip(values, -reach, reach).astype(held_as)


def setup_inputs(seed: int = 0) -> dict:
    keys = jax.random.split(jax.random.key(seed), 8)
    return {
        "sky_image": scatter_about(keys[0], (C, N, N), 1.0, 6.0, ((0, 2), (1, 64)), jnp.float32),
        "fourier_dual": scatter_about(keys[1], (2, C, N, N), 1.0, 6.0, ((1, 2), (2, 64)), jnp.float32),
        "visibilities": draw_visibilities(jax.random.fold_in(keys[7], 71), 0),
        "weights": jnp.clip(jnp.exp(math.log(1.0) - 2.3025851 * jax.random.uniform(keys[3], (C, N, N), jnp.float32) ** block_scale(keys[3], (C, N, N), ((0, 2), (1, 64)), -0.2, 0.2)), 0.1, 1.0),
        "radius": jnp.clip(0.2 + 0.400000021 * jax.random.uniform(keys[4], (C,), jnp.float32) ** block_scale(keys[4], (C,), ((0, 2),), -0.2, 0.2), 0.2, 0.6),
        "wavelet_dual": scatter_about(keys[5], (C, N, N), 1.0, 6.0, ((1, 128),), jnp.float32),
        "reweight": jnp.clip(jnp.exp(math.log(3.0) - 2.3025851 * jax.random.uniform(keys[6], (N, N), jnp.float32) ** block_scale(keys[6], (N, N), ((0, 128),), -0.2, 0.2)), 0.3, 3.0),
    }


data_step = 0.8
primal_step = 0.5
low_taps = (0.0625, 0.25, 0.375, 0.25, 0.0625)
high_taps = (-0.1, -0.3, 0.7, -0.2, -0.1)
low_reverse = (0.0625, 0.25, 0.375, 0.25, 0.0625)
high_reverse = (-0.1, -0.2, 0.7, -0.3, -0.1)

def filter_rows(extended, filter_taps):
    count_rows = extended.shape[1] - 4
    total = filter_taps[0] * extended[:, 0:count_rows]
    for offset in range(1, 5):
        total = total + filter_taps[offset] * extended[:, offset:offset + count_rows]
    return total

def filter_columns(values, filter_taps):
    count_cols = values.shape[2]
    padded = jnp.pad(values, ((0, 0), (0, 0), (2, 2)))
    total = filter_taps[0] * padded[:, :, 0:count_cols]
    for offset in range(1, 5):
        total = total + filter_taps[offset] * padded[:, :, offset:offset + count_cols]
    return total

def analysis(extended, low_set, high_set):
    return filter_columns(filter_rows(extended, high_set), low_set) + filter_columns(filter_rows(extended, low_set), high_set)

def soft_dual(combined, threshold):
    magnitude = jnp.sqrt(lax.optimization_barrier(jnp.sum(combined * combined, axis=0)))
    return combined * (threshold / jnp.maximum(magnitude, threshold))

def reference(sky_image, fourier_dual, visibilities, weights, radius, wavelet_dual, reweight):
    side = sky_image.shape[1]
    spectrum = jnp.swapaxes(jnp.fft.fft2(sky_image), 1, 2) / side
    resid_re = fourier_dual[0] / data_step + weights * jnp.real(spectrum) - visibilities[0]
    resid_im = fourier_dual[1] / data_step + weights * jnp.imag(spectrum) - visibilities[1]
    resid_norm = lax.optimization_barrier(jnp.sum(resid_re * resid_re + resid_im * resid_im, axis=(1, 2)))
    data_norm = lax.optimization_barrier(jnp.sum(visibilities[0] * visibilities[0] + visibilities[1] * visibilities[1], axis=(1, 2)))
    shrink = data_step * (1.0 - radius * jnp.sqrt(data_norm) / jnp.sqrt(resid_norm))
    new_re = resid_re * shrink[:, None, None]
    new_im = resid_im * shrink[:, None, None]
    fourier_new = jnp.stack([new_re, new_im])
    weighted = lax.complex(weights * new_re, weights * new_im)
    gradient = jnp.real(jnp.fft.ifft2(jnp.swapaxes(weighted, 1, 2))) * side
    extended = jnp.pad(sky_image, ((0, 0), (2, 2), (0, 0)))
    combined = wavelet_dual + analysis(extended, low_taps, high_taps)
    wavelet_new = soft_dual(combined, reweight)
    adjoint = analysis(jnp.pad(wavelet_new, ((0, 0), (2, 2), (0, 0))), low_reverse, high_reverse)
    image_new = jnp.maximum(sky_image - primal_step * (gradient + adjoint), 0.0)
    return (image_new, fourier_new, wavelet_new)
```

```python
import math

import jax
import jax.numpy as jnp
import numpy as np
from jax import lax
from jax.experimental import pallas as pl
from jax.experimental.pallas import tpu as pltpu
from jax.sharding import PartitionSpec as P

data_step = 0.8
primal_step = 0.5
low_taps = (0.0625, 0.25, 0.375, 0.25, 0.0625)
high_taps = (-0.1, -0.3, 0.7, -0.2, -0.1)
low_reverse = (0.0625, 0.25, 0.375, 0.25, 0.0625)
high_reverse = (-0.1, -0.2, 0.7, -0.3, -0.1)

SIDE = 4096
RADIX = 32
WIDE = 128


def over_copies(array, axis):
    count = lax.axis_size(axis)
    sent = jnp.broadcast_to(array[None], (count, *array.shape))
    return lax.all_to_all(sent, axis, 0, 0, tiled=True).sum(axis=0)


def extended_2(array, sides, width):
    edges = {}
    for axis, dim in sides:
        count, length = (lax.axis_size(axis), array.shape[dim])
        up = [(i, (i + 1) % count) for i in range(count - 1)]
        last = lax.slice_in_dim(array, length - width, length, axis=dim)
        first = lax.slice_in_dim(array, 0, width, axis=dim)
        edges[dim] = (
            lax.ppermute(last, axis, up),
            lax.ppermute(first, axis, [(b, a) for a, b in up]),
        )
    for _, dim in sides:
        low, high = edges[dim]
        array = jnp.concatenate([low, array, high], axis=dim)
    return array


def filter_rows(extended, filter_taps):
    count_rows = extended.shape[1] - 4
    total = filter_taps[0] * extended[:, 0:count_rows]
    for offset in range(1, 5):
        total = total + filter_taps[offset] * extended[:, offset : offset + count_rows]
    return total


def filter_columns(values, filter_taps):
    count_cols = values.shape[2]
    padded = jnp.pad(values, ((0, 0), (0, 0), (2, 2)))
    total = filter_taps[0] * padded[:, :, 0:count_cols]
    for offset in range(1, 5):
        total = total + filter_taps[offset] * padded[:, :, offset : offset + count_cols]
    return total


def analysis(extended, low_set, high_set):
    return filter_columns(filter_rows(extended, high_set), low_set) + filter_columns(
        filter_rows(extended, low_set), high_set
    )


def soft_dual(combined, threshold):
    magnitude = jnp.sqrt(jnp.sum(combined * combined, axis=0))
    return combined * (threshold / jnp.maximum(magnitude, threshold))


def c_add(a, b):
    re = a[0] + b[0]
    if a[1] is None:
        return (re, b[1])
    return (re, a[1] if b[1] is None else a[1] + b[1])


def c_sub(a, b):
    re = a[0] - b[0]
    if a[1] is None:
        return (re, None if b[1] is None else -b[1])
    return (re, a[1] if b[1] is None else a[1] - b[1])


def c_turn(a, k, n, orient):
    re, im = a
    if k == 0:
        return a
    if 4 * k == n:
        if im is None:
            return (None, re if orient > 0 else -re)
        return (-im, re) if orient > 0 else (im, -re)
    cos, sin = math.cos(2 * math.pi * k / n), orient * math.sin(2 * math.pi * k / n)
    if im is None:
        return (re * cos, re * sin)
    if 8 * k == n:
        return ((re - im) * cos, (re + im) * cos) if orient > 0 else ((re + im) * cos, (im - re) * cos)
    if 8 * k == 3 * n:
        c = -cos
        return ((-re - im) * c, (re - im) * c) if orient > 0 else ((im - re) * c, (-re - im) * c)
    return (re * cos - im * sin, re * sin + im * cos)


def short_fft(items, orient):
    n = len(items)
    if n == 1:
        return list(items)
    even = short_fft(items[0::2], orient)
    odd = short_fft(items[1::2], orient)
    low, high = [], []
    for k in range(n // 2):
        if even[k][1] is None and odd[k][1] is None and 4 * k == n:
            low.append((even[k][0], orient * odd[k][0]))
            high.append((even[k][0], -orient * odd[k][0]))
            continue
        turned = c_turn(odd[k], k, n, orient)
        low.append(c_add(even[k], turned))
        high.append(c_sub(even[k], turned))
    return low + high


def dft_matrix(orient):
    idx = np.arange(WIDE)
    angle = 2 * np.pi * ((idx[:, None] * idx[None, :]) % WIDE) / WIDE
    cos, sin = np.cos(angle) / 64.0, orient * np.sin(angle) / 64.0
    return np.block([[cos, sin], [-sin, cos]])


def halves_first(matrix_rows):
    order = np.arange(WIDE).reshape(64, 2).T.reshape(-1)
    return np.concatenate([matrix_rows[:WIDE][order], matrix_rows[WIDE:][order]])


def high_low(matrix):

    bf = np.asarray(matrix, np.float32).astype(jnp.bfloat16)
    low = (np.asarray(matrix) - bf.astype(np.float64)).astype(jnp.bfloat16)
    return (jnp.asarray(np.stack([bf, low])),)


def twiddle(orient):
    angle = 2 * np.pi * (np.arange(RADIX)[:, None] * np.arange(WIDE)[None, :]) / SIDE
    return jnp.asarray(np.stack([np.cos(angle), orient * np.sin(angle)]), jnp.float32)


def split_two(x):
    high = x.astype(jnp.bfloat16)
    return high, (x - high.astype(jnp.float32)).astype(jnp.bfloat16)


def product(dims, a_pair, b_pair):
    def one(a, b):
        return lax.dot_general(a, b, (dims, ((), ())), preferred_element_type=jnp.float32)

    return one(a_pair[0], b_pair[0]) + (one(a_pair[1], b_pair[0]) + one(a_pair[0], b_pair[1]))


def spread(matrix_ref, block):
    return product(((1,), (1,)), (matrix_ref[0], matrix_ref[1]), split_two(block))


def gather(block, matrix_ref):
    return product(((0,), (0,)), split_two(block), (matrix_ref[0], matrix_ref[1]))


def c_mul(a, b_re, b_im):
    return (a[0] * b_re - a[1] * b_im, a[0] * b_im + a[1] * b_re)


def rows_forward(x_ref, tw_ref, matrix_ref, out_ref, held):
    def short(at, _):
        items = [(x_ref[at, p], None) for p in range(RADIX)]
        done = short_fft(items, -1)
        a_hi, a_mid = at // 2, at % 2
        for q in range(RADIX):
            value = done[q]
            if value[1] is None:
                re = value[0] * tw_ref[0, pl.ds(q, 1), :]
                im = value[0] * tw_ref[1, pl.ds(q, 1), :]
            else:
                re, im = c_mul(value, tw_ref[0, pl.ds(q, 1), :], tw_ref[1, pl.ds(q, 1), :])
            row = pl.ds(pl.multiple_of((q % 8) * 16 + a_mid * 8, 8), 8)
            held[(q // 8) * 4 + a_hi, row, 0:WIDE] = re
            held[(q // 8) * 4 + a_hi, row, WIDE:] = im
        return 0

    lax.fori_loop(0, 8, short, 0)

    def long(block, _):
        q_hi, a_hi = block // 4, block % 4
        result = spread(matrix_ref, held[block])
        for c in range(2):
            for e in range(2):
                for d in range(0, 64, 8):
                    start = d * 64 + c * 32 + e * 4 + a_hi * 8 + q_hi
                    m = c * 128 + e * 64 + d
                    out_ref[pl.ds(start, 8, stride=64), :] = result[m : m + 8]
        return 0

    lax.fori_loop(0, 16, long, 0)


def columns_both(
    in_ref, dual_ref, vis_ref, weight_ref, tw_ref, to_ref, back_ref,
    resid_ref, out_ref, sums_ref, wide, held,
):
    def long(block, _):
        l_hi, q_hi = block // 8, block % 8
        rows = []
        for c in range(2):
            for jh in range(2):
                rows.append(in_ref[pl.ds(c * 32 + jh * 16 + l_hi * 8 + q_hi, 64, stride=64), :])
        result = gather(jnp.concatenate(rows), to_ref)
        for q_lo in range(8):
            row = pl.ds(pl.multiple_of((q_hi * 8 + q_lo) * 32 + l_hi * 16, 8), 16)
            wide[0, row, :] = result[q_lo * 16 : q_lo * 16 + 16, 0:WIDE]
            wide[1, row, :] = result[q_lo * 16 : q_lo * 16 + 16, WIDE:]
        return 0

    lax.fori_loop(0, 16, long, 0)
    sums_ref[...] = jnp.zeros_like(sums_ref)

    def short(q_hi, _):
        items = []
        for l in range(RADIX):
            row = pl.ds(q_hi * 256 + l, 8, stride=32)
            items.append(
                c_mul((wide[0, row, :], wide[1, row, :]), tw_ref[0, pl.ds(l, 1), :], tw_ref[1, pl.ds(l, 1), :])
            )
        freq = short_fft(items, -1)
        total = sums_ref[0]
        total_vis = sums_ref[1]
        items = []
        for v in range(RADIX):
            weight = weight_ref[q_hi, v]
            vis_re, vis_im = vis_ref[0, q_hi, v], vis_ref[1, q_hi, v]
            re = dual_ref[0, q_hi, v] * (1.0 / data_step) + weight * freq[v][0] - vis_re
            im = dual_ref[1, q_hi, v] * (1.0 / data_step) + weight * freq[v][1] - vis_im
            total = total + (re * re + im * im)
            total_vis = total_vis + (vis_re * vis_re + vis_im * vis_im)
            resid_ref[0, q_hi, v] = re
            resid_ref[1, q_hi, v] = im
            items.append((weight * re, weight * im))
        sums_ref[0] = total
        sums_ref[1] = total_vis
        done = short_fft(items, 1)
        for l in range(RADIX):
            re, im = c_mul(done[l], tw_ref[0, pl.ds(l, 1), :], -tw_ref[1, pl.ds(l, 1), :])
            row = pl.ds((l % 16) * 8, 8)
            held[(l // 16) * 8 + q_hi, row, 0:WIDE] = re
            held[(l // 16) * 8 + q_hi, row, WIDE:] = im
        return 0

    lax.fori_loop(0, 8, short, 0)

    def long_back(block, _):
        l_hi, q_hi = block // 8, block % 8
        result = spread(back_ref, held[block])
        for c in range(2):
            for jh in range(2):
                for s in range(0, 64, 8):
                    start = s * 64 + c * 32 + jh * 16 + l_hi * 8 + q_hi
                    m = c * 128 + jh * 64 + s
                    out_ref[pl.ds(start, 8, stride=64), :] = result[m : m + 8]
        return 0

    lax.fori_loop(0, 16, long_back, 0)


def rows_back(shrink_ref, in_ref, x_ref, adjoint_ref, tw_ref, matrix_ref, out_ref, wide):
    def long(block, _):
        a_hi, q_hi = block // 4, block % 4
        rows = []
        for c in range(2):
            for e in range(2):
                rows.append(in_ref[pl.ds(c * 32 + a_hi * 8 + e * 4 + q_hi, 64, stride=64), :])
        result = gather(jnp.concatenate(rows), matrix_ref)
        for a_lo in range(16):
            row = pl.ds(pl.multiple_of((a_hi * 16 + a_lo) * 32 + q_hi * 8, 8), 8)
            wide[0, row, :] = result[a_lo * 8 : a_lo * 8 + 8, 0:WIDE]
            wide[1, row, :] = result[a_lo * 8 : a_lo * 8 + 8, WIDE:]
        return 0

    lax.fori_loop(0, 16, long, 0)
    shrink = shrink_ref[0]

    def short(at, _):
        items = []
        for q in range(RADIX):
            row = pl.ds(at * 256 + q, 8, stride=32)
            items.append(
                c_mul((wide[0, row, :], wide[1, row, :]), tw_ref[0, pl.ds(q, 1), :], -tw_ref[1, pl.ds(q, 1), :])
            )
        done = short_fft(items, 1)
        for p in range(RADIX):
            step = done[p][0] * shrink + adjoint_ref[at, p]
            out_ref[at, p] = jnp.maximum(x_ref[at, p] - primal_step * step, 0.0)
        return 0

    lax.fori_loop(0, 8, short, 0)


def tiles(array):
    lead = array.shape[:-2]
    array = array.reshape(lead + (8, 8, 32, 128))
    n = len(lead)
    return array.transpose(tuple(range(n)) + (n, n + 2, n + 1, n + 3))


def untiles(array):
    n = array.ndim - 4
    array = array.transpose(tuple(range(n)) + (n, n + 2, n + 1, n + 3))
    return array.reshape(array.shape[:n] + (64, SIDE))


TILES = (8, 32, 8, 128)
VMEM_SPEC = pl.BlockSpec(memory_space=pltpu.VMEM)
F32 = jnp.float32


def per_device(sky_image, fourier_dual, visibilities, weights, radius, wavelet_dual, reweight):
    tw = twiddle(-1.0)
    forward, backward = dft_matrix(-1.0), dft_matrix(1.0)
    spread_rows = high_low(halves_first(forward.T))[0]
    gather_cols = high_low(halves_first(forward))[0]
    spread_cols = high_low(halves_first(backward.T))[0]
    gather_rows = high_low(halves_first(backward))[0]
    params = pltpu.CompilerParams(vmem_limit_bytes=48 << 20)

    x_tiles = tiles(sky_image[0])
    sent = pl.pallas_call(
        rows_forward,
        out_shape=jax.ShapeDtypeStruct((4096, 128), F32),
        in_specs=[VMEM_SPEC] * 3,
        out_specs=VMEM_SPEC,
        scratch_shapes=[pltpu.VMEM((16, 128, 256), F32)],
        compiler_params=params,
        cost_estimate=pl.CostEstimate(flops=8 << 27, bytes_accessed=4 << 20, transcendentals=0),
    )(x_tiles, tw, spread_rows)
    arrived = lax.all_to_all(sent.reshape(64, 64, 128), "row", 0, 0, tiled=True).reshape(4096, 128)
    resid, outgoing, sums = pl.pallas_call(
        columns_both,
        out_shape=(
            jax.ShapeDtypeStruct((2, *TILES), F32),
            jax.ShapeDtypeStruct((4096, 128), F32),
            jax.ShapeDtypeStruct((2, 8, 128), F32),
        ),
        in_specs=[VMEM_SPEC] * 7,
        out_specs=(VMEM_SPEC,) * 3,
        scratch_shapes=[pltpu.VMEM((2, 2048, 128), F32), pltpu.VMEM((16, 128, 256), F32)],
        compiler_params=params,
        cost_estimate=pl.CostEstimate(flops=16 << 27, bytes_accessed=12 << 20, transcendentals=0),
    )(
        arrived, tiles(fourier_dual[:, 0]), tiles(visibilities[:, 0]), tiles(weights[0]), tw,
        gather_cols, spread_cols,
    )
    returned = lax.all_to_all(outgoing.reshape(64, 64, 128), "row", 0, 0, tiled=True).reshape(4096, 128)
    norms = over_copies(jnp.sum(sums, axis=(1, 2)), "row")
    shrink = data_step * (1.0 - radius * jnp.sqrt(norms[1]) / jnp.sqrt(norms[0]))
    fourier_new = untiles(resid * shrink[0])[:, None]

    facet_image = lax.all_to_all(sky_image, "chan", split_axis=1, concat_axis=0, tiled=True)
    channels = facet_image.shape[0]
    rows_facet = facet_image.shape[1]
    bundle = jnp.concatenate([facet_image, wavelet_dual, reweight[None]], axis=0)
    extended = extended_2(bundle, ((("row", "chan"), 1),), 4)
    combined = extended[channels : 2 * channels, 2:-2] + analysis(
        extended[:channels], low_taps, high_taps
    )
    offset_row = lax.axis_index(("row", "chan")) * rows_facet - 2
    positions = offset_row + jnp.arange(rows_facet + 4, dtype=jnp.int32)
    total_rows = rows_facet * lax.axis_size(("row", "chan"))
    inside = (positions >= 0) & (positions < total_rows)
    threshold = jnp.where(inside[:, None], extended[2 * channels, 2:-2], 1.0)
    wide_new = jnp.where(inside[None, :, None], soft_dual(combined, threshold), 0.0)
    wavelet_new = wide_new[:, 2:-2]
    adjoint = analysis(wide_new, low_reverse, high_reverse)
    adjoint_rows = lax.all_to_all(adjoint, "chan", split_axis=0, concat_axis=1, tiled=True)

    image = pl.pallas_call(
        rows_back,
        out_shape=jax.ShapeDtypeStruct(TILES, F32),
        in_specs=[pl.BlockSpec(memory_space=pltpu.SMEM)] + [VMEM_SPEC] * 5,
        out_specs=VMEM_SPEC,
        scratch_shapes=[pltpu.VMEM((2, 2048, 128), F32)],
        compiler_params=params,
        cost_estimate=pl.CostEstimate(flops=8 << 27, bytes_accessed=5 << 20, transcendentals=0),
    )(shrink, returned, x_tiles, tiles(adjoint_rows[0]), tw, gather_rows)
    return (untiles(image)[None], fourier_new, wavelet_new)


def solution(mesh):
    in_specs = (
        P("chan", "row", None),
        P(None, "chan", "row", None),
        P(None, "chan", "row", None),
        P("chan", "row", None),
        P("chan"),
        P(None, ("row", "chan"), None),
        P(("row", "chan"), None),
    )
    out_specs = (
        P("chan", "row", None),
        P(None, "chan", "row", None),
        P(None, ("row", "chan"), None),
    )
    return jax.shard_map(
        per_device, mesh=mesh, in_specs=in_specs, out_specs=out_specs, check_vma=False
    )
```

```python
import math

import jax
import jax.numpy as jnp
import numpy as np
from jax import lax
from jax.experimental import pallas as pl
from jax.experimental.pallas import tpu as pltpu
from jax.sharding import PartitionSpec as P

data_step = 0.8
primal_step = 0.5
low_taps = (0.0625, 0.25, 0.375, 0.25, 0.0625)
high_taps = (-0.1, -0.3, 0.7, -0.2, -0.1)
low_reverse = (0.0625, 0.25, 0.375, 0.25, 0.0625)
high_reverse = (-0.1, -0.2, 0.7, -0.3, -0.1)

F32 = jnp.float32
SIDE = 4096
RADIX = 32
WIDE = 128


def c_add(a, b):
    re = a[0] + b[0]
    if a[1] is None:
        return (re, b[1])
    return (re, a[1] if b[1] is None else a[1] + b[1])


def c_sub(a, b):
    re = a[0] - b[0]
    if a[1] is None:
        return (re, None if b[1] is None else -b[1])
    return (re, a[1] if b[1] is None else a[1] - b[1])


def c_turn(a, k, n, orient):
    re, im = a
    if k == 0:
        return a
    if 4 * k == n:
        if im is None:
            return (None, re if orient > 0 else -re)
        return (-im, re) if orient > 0 else (im, -re)
    cos, sin = math.cos(2 * math.pi * k / n), orient * math.sin(2 * math.pi * k / n)
    if im is None:
        return (re * cos, re * sin)
    if 8 * k == n:
        return ((re - im) * cos, (re + im) * cos) if orient > 0 else ((re + im) * cos, (im - re) * cos)
    if 8 * k == 3 * n:
        c = -cos
        return ((-re - im) * c, (re - im) * c) if orient > 0 else ((im - re) * c, (-re - im) * c)
    return (re * cos - im * sin, re * sin + im * cos)


def short_fft(items, orient):
    n = len(items)
    if n == 1:
        return list(items)
    even = short_fft(items[0::2], orient)
    odd = short_fft(items[1::2], orient)
    low, high = [], []
    for k in range(n // 2):
        if even[k][1] is None and odd[k][1] is None and 4 * k == n:
            low.append((even[k][0], orient * odd[k][0]))
            high.append((even[k][0], -orient * odd[k][0]))
            continue
        turned = c_turn(odd[k], k, n, orient)
        low.append(c_add(even[k], turned))
        high.append(c_sub(even[k], turned))
    return low + high


def dft_matrix(orient):
    idx = np.arange(WIDE)
    angle = 2 * np.pi * ((idx[:, None] * idx[None, :]) % WIDE) / WIDE
    cos, sin = np.cos(angle) / 64.0, orient * np.sin(angle) / 64.0
    return np.block([[cos, sin], [-sin, cos]])


def halves_first(matrix_rows):
    order = np.arange(WIDE).reshape(64, 2).T.reshape(-1)
    return np.concatenate([matrix_rows[:WIDE][order], matrix_rows[WIDE:][order]])


def high_low(matrix):

    bf = np.asarray(matrix, np.float32).astype(jnp.bfloat16)
    low = (np.asarray(matrix) - bf.astype(np.float64)).astype(jnp.bfloat16)
    return (jnp.asarray(np.stack([bf, low])),)


def twiddle(orient):
    angle = 2 * np.pi * (np.arange(RADIX)[:, None] * np.arange(WIDE)[None, :]) / SIDE
    return jnp.asarray(np.stack([np.cos(angle), orient * np.sin(angle)]), jnp.float32)


def split_two(x):
    high = x.astype(jnp.bfloat16)
    return high, (x - high.astype(jnp.float32)).astype(jnp.bfloat16)


def product(dims, a_pair, b_pair):
    def one(a, b):
        return lax.dot_general(a, b, (dims, ((), ())), preferred_element_type=jnp.float32)

    return one(a_pair[0], b_pair[0]) + (one(a_pair[1], b_pair[0]) + one(a_pair[0], b_pair[1]))


def spread(matrix_ref, block):
    return product(((1,), (1,)), (matrix_ref[0], matrix_ref[1]), split_two(block))


def gather(block, matrix_ref):
    return product(((0,), (0,)), split_two(block), (matrix_ref[0], matrix_ref[1]))


def c_mul(a, b_re, b_im):
    return (a[0] * b_re - a[1] * b_im, a[0] * b_im + a[1] * b_re)


MESH = pl.DeviceIdType.MESH
PEERS = 64
CHUNK = 64
PIECE = 16
PIECES = 4
PRIOR_AFTER = 1


def chunk_row(g, c, a_hi, e):
    return g * PIECE + c * 8 + a_hi * 2 + e


def step(
    radius_ref, x_hbm, dual_hbm, vis_hbm, weight_hbm, prior_hbm, limit_hbm, tw_ref, sr_ref, gc_ref, sc_ref, gr_ref,
    image_ref, fourier_ref, wavelet_ref,
    x_ref, dual_ref, vis_ref, weight_ref, prior_ref, limit_ref,
    sent, arrived, sent_back, returned, held, wide, sums, own_sums, all_sums,
    near_send, far_send, sky_got, near_got, far_got, grown, edge_send, prior_got, edge_got, spread_new,
    load_sem, own_sem, send_sem, recv_sem, back_send, back_recv, sum_send, sum_recv, sky_send, sky_recv, pri_send, pri_recv,
):
    r, ch = lax.axis_index("row"), lax.axis_index("chan")
    other = 1 - ch
    after, before = lax.rem(r + 1, PEERS), lax.rem(r + PEERS - 1, PEERS)

    loads = [
        pltpu.make_async_copy(src, dst, load_sem.at[i])
        for i, (src, dst) in enumerate(
            (
                (x_hbm, x_ref), (prior_hbm, prior_ref), (limit_hbm, limit_ref),
                (dual_hbm, dual_ref), (vis_hbm, vis_ref), (weight_hbm, weight_ref),
            )
        )
    ]
    for load in loads:
        load.start()

    barrier = pltpu.get_barrier_semaphore()

    def greet(i, _):
        pl.semaphore_signal(barrier, inc=1, device_id=(lax.rem(r + i, PEERS), ch), device_id_type=MESH)
        return 0

    lax.fori_loop(1, PEERS, greet, 0)
    for row in (r, after, before):
        pl.semaphore_signal(barrier, inc=1, device_id=(row, other), device_id_type=MESH)

    def remote(src, dst, send, recv, row, chan):
        return pltpu.make_async_remote_copy(
            src_ref=src, dst_ref=dst, send_sem=send, recv_sem=recv, device_id=(row, chan), device_id_type=MESH
        )

    loads[0].wait()

    def row_short(at, _):
        items = [(x_ref[at, p], None) for p in range(RADIX)]
        done = short_fft(items, -1)
        a_hi, a_mid = at // 2, at % 2
        for q in range(RADIX):
            value = done[q]
            if value[1] is None:
                re = value[0] * tw_ref[0, pl.ds(q, 1), :]
                im = value[0] * tw_ref[1, pl.ds(q, 1), :]
            else:
                re, im = c_mul(value, tw_ref[0, pl.ds(q, 1), :], tw_ref[1, pl.ds(q, 1), :])
            row = pl.ds(pl.multiple_of((q % 8) * 16 + a_mid * 8, 8), 8)
            held[(q // 8) * 4 + a_hi, row, 0:WIDE] = re
            held[(q // 8) * 4 + a_hi, row, WIDE:] = im
        return 0

    lax.fori_loop(0, 8, row_short, 0)

    first_here = ch == 0

    def edges(t, _):
        low, high = x_ref[4, t][0:2], x_ref[3, t][6:8]
        near_send[t] = jnp.where(first_here, high, low)
        far_send[0, t] = x_ref[7, t][6:8]
        far_send[1, t] = x_ref[0, t][0:2]
        return 0

    lax.fori_loop(0, 32, edges, 0)
    pl.semaphore_wait(barrier, PEERS + 2)

    half = pl.ds(pl.multiple_of(other * 4, 4), 4)
    sky_copies = [
        remote(x_ref.at[half], sky_got, sky_send.at[0], sky_recv.at[0], r, other),
        remote(near_send, near_got, sky_send.at[1], sky_recv.at[1], r, other),
    ]
    for copy in sky_copies:
        copy.start()
    far_up = remote(far_send.at[0], far_got.at[ch], sky_send.at[2], sky_recv.at[2 + ch], after, 0)
    far_down = remote(far_send.at[1], far_got.at[ch], sky_send.at[3], sky_recv.at[2 + ch], before, 1)
    far_up.start()
    far_down.start()

    def piece_copies(src, dst, send, recv, g):
        def one(i, _):
            d = lax.rem(r + i, PEERS)
            take = pl.ds(pl.multiple_of(d * CHUNK + g * PIECE, PIECE), PIECE)
            give = pl.ds(pl.multiple_of(r * CHUNK + g * PIECE, PIECE), PIECE)
            remote(src.at[take], dst.at[give], send.at[g], recv.at[g], d, ch).start()
            return 0

        lax.fori_loop(1, PEERS, one, 0)
        mine = pl.ds(pl.multiple_of(r * CHUNK + g * PIECE, PIECE), PIECE)
        return pltpu.make_async_copy(src.at[mine], dst.at[mine], own_sem)

    def all_of(src, dst, send, recv, g):
        rows = pl.ds(0, (PEERS - 1) * PIECE)
        return remote(src.at[rows], dst.at[rows], send.at[g], recv.at[g], after, ch)

    def row_piece(g, _):
        def block(a_hi, _):
            result = spread(sr_ref, held[g * 4 + a_hi])
            for c in range(2):
                for e in range(2):
                    for d in range(0, 64, 8):
                        m = c * 128 + e * 64 + d
                        sent[pl.ds(d * CHUNK + chunk_row(g, c, a_hi, e), 8, stride=CHUNK), :] = result[m : m + 8]
            return 0

        lax.fori_loop(0, 4, block, 0)
        own = piece_copies(sent, arrived, send_sem, recv_sem, g)
        own.start()
        own.wait()
        return 0

    lax.fori_loop(0, PIECES, row_piece, 0)

    for load in loads[3:]:
        load.wait()
    sums[...] = jnp.zeros_like(sums)

    def column_piece(g, _):
        all_of(sent, arrived, send_sem, recv_sem, g).wait_recv()

        def block(i, _):
            l_hi, e = i // 2, i % 2
            rows = []
            for c in range(2):
                for jh in range(2):
                    rows.append(arrived[pl.ds(chunk_row(g, c, jh * 2 + l_hi, e), PEERS, stride=CHUNK), :])
            result = gather(jnp.concatenate(rows), gc_ref)
            for q_lo in range(8):
                row = pl.ds(pl.multiple_of(((e * 4 + g) * 8 + q_lo) * 32 + l_hi * 16, 16), 16)
                wide[0, row, :] = result[q_lo * 16 : q_lo * 16 + 16, 0:WIDE]
                wide[1, row, :] = result[q_lo * 16 : q_lo * 16 + 16, WIDE:]
            return 0

        lax.fori_loop(0, 4, block, 0)

        def short(e, _):
            q_hi = e * 4 + g
            items = []
            for l in range(RADIX):
                row = pl.ds(q_hi * 256 + l, 8, stride=32)
                items.append(
                    c_mul((wide[0, row, :], wide[1, row, :]), tw_ref[0, pl.ds(l, 1), :], tw_ref[1, pl.ds(l, 1), :])
                )
            freq = short_fft(items, -1)
            total, total_vis = sums[0], sums[1]
            items = []
            for v in range(RADIX):
                weight = weight_ref[q_hi, v]
                vis_re, vis_im = vis_ref[0, q_hi, v], vis_ref[1, q_hi, v]
                re = dual_ref[0, q_hi, v] * (1.0 / data_step) + weight * freq[v][0] - vis_re
                im = dual_ref[1, q_hi, v] * (1.0 / data_step) + weight * freq[v][1] - vis_im
                total = total + (re * re + im * im)
                total_vis = total_vis + (vis_re * vis_re + vis_im * vis_im)
                fourier_ref[0, q_hi, v] = re
                fourier_ref[1, q_hi, v] = im
                items.append((weight * re, weight * im))
            sums[0] = total
            sums[1] = total_vis
            done = short_fft(items, 1)
            for l in range(RADIX):
                re, im = c_mul(done[l], tw_ref[0, pl.ds(l, 1), :], -tw_ref[1, pl.ds(l, 1), :])
                row = pl.ds((l % 16) * 8, 8)
                held[(l // 16) * 8 + q_hi, row, 0:WIDE] = re
                held[(l // 16) * 8 + q_hi, row, WIDE:] = im
            return 0

        lax.fori_loop(0, 2, short, 0)

        def block_back(i, _):
            l_hi, e = i // 2, i % 2
            result = spread(sc_ref, held[l_hi * 8 + e * 4 + g])
            for c in range(2):
                for jh in range(2):
                    for s in range(0, 64, 8):
                        m = c * 128 + jh * 64 + s
                        start = s * CHUNK + chunk_row(g, c, jh * 2 + l_hi, e)
                        sent_back[pl.ds(start, 8, stride=CHUNK), :] = result[m : m + 8]
            return 0

        lax.fori_loop(0, 4, block_back, 0)
        own = piece_copies(sent_back, returned, back_send, back_recv, g)
        own.start()
        own.wait()
        return 0

    lane = lax.broadcasted_iota(jnp.int32, (8, 128), 1)

    def filter_column(load, low_set, high_set, carry):
        taps = [load(p) for p in range(5)]
        low = taps[0] * low_set[0]
        high = taps[0] * high_set[0]
        for p in range(1, 5):
            low = low + taps[p] * low_set[p]
            high = high + taps[p] * high_set[p]
        return finish_column(low, high, low_set, high_set, carry)

    def finish_column(low, high, low_set, high_set, carry):
        old0, old1, unfinished = carry
        terms = [high * low_set[p] + low * high_set[p] for p in range(5)]
        new0 = pltpu.roll(terms[0], 2, 1)
        new1 = pltpu.roll(terms[1], 1, 1)
        new3 = pltpu.roll(terms[3], 127, 1)
        new4 = pltpu.roll(terms[4], 126, 1)
        finished = unfinished + jnp.where(lane >= 127, new3, 0.0) + jnp.where(lane >= 126, new4, 0.0)
        started = (
            terms[2]
            + (jnp.where(lane >= 2, new0, old0) + jnp.where(lane >= 1, new1, old1))
            + (jnp.where(lane < 127, new3, 0.0) + jnp.where(lane < 126, new4, 0.0))
        )
        return finished, (new0, new1, started)

    zero = jnp.zeros((8, 128), F32)
    prior_copies = [
        remote(wavelet_ref.at[other], prior_got, pri_send.at[0], pri_recv.at[0], r, other)
    ] + [
        remote(
            edge_send.at[c], edge_got.at[1 - ch], pri_send.at[1 + c], pri_recv.at[2 - ch],
            lax.rem(r + PEERS - 1 + 2 * ch, PEERS), c,
        )
        for c in range(2)
    ]

    def prior_step():
        for load in loads[1:3]:
            load.wait()
        for copy in sky_copies:
            copy.wait_recv()
        for k in range(2):
            remote(far_send.at[0], far_got.at[k], sky_send.at[2], sky_recv.at[2 + k], r, other).wait_recv()
        no_far = jnp.logical_or(
            jnp.logical_and(ch == 0, r == 0), jnp.logical_and(ch == 1, r == PEERS - 1)
        )

        def grow(t, _):
            for k in range(4):
                grown[ch, t, 8 + 8 * k : 16 + 8 * k, :] = x_ref[ch * 4 + k, t]
                grown[other, t, 8 + 8 * k : 16 + 8 * k, :] = sky_got[k, t]
            near_own = jnp.where(first_here, x_ref[4, t][0:2], x_ref[3, t][6:8])
            near_other = near_got[t]
            far_own = jnp.where(no_far, 0.0, far_got[ch, t])
            far_other = jnp.where(no_far, 0.0, far_got[other, t])
            grown[ch, t, 6:8, :] = jnp.where(first_here, far_own, near_own)
            grown[ch, t, 40:42, :] = jnp.where(first_here, near_own, far_own)
            grown[other, t, 6:8, :] = jnp.where(first_here, far_other, near_other)
            grown[other, t, 40:42, :] = jnp.where(first_here, near_other, far_other)
            return 0

        lax.fori_loop(0, 32, grow, 0)

        def close(t, filtered):
            for k in range(4):
                s0 = prior_ref[0, k, t] + filtered[0][k]
                s1 = prior_ref[1, k, t] + filtered[1][k]
                limit = limit_ref[k, t]
                scale = limit / jnp.maximum(jnp.sqrt(s0 * s0 + s1 * s1), limit)
                wavelet_ref[0, k, t] = s0 * scale
                wavelet_ref[1, k, t] = s1 * scale

        def columns(t, carry):
            filtered, new = [[], []], []
            for c in range(2):
                for k in range(4):
                    finished, kept = filter_column(
                        lambda p: grown[c, t, 6 + 8 * k + p : 14 + 8 * k + p, :], low_taps, high_taps, carry[c * 4 + k]
                    )
                    filtered[c].append(finished)
                    new.append(kept)
            close(jnp.maximum(t - 1, 0), filtered)
            return tuple(new)

        carry = lax.fori_loop(0, 32, columns, ((zero, zero, zero),) * 8)
        close(31, [[carry[c * 4 + k][2] for k in range(4)] for c in range(2)])

        def edge(t, _):
            for c in range(2):
                edge_send[c, t] = jnp.where(
                    first_here, wavelet_ref[c, 0, t][0:2], wavelet_ref[c, 3, t][6:8]
                )
            return 0

        lax.fori_loop(0, 32, edge, 0)

        for copy in prior_copies:
            copy.start()


    def adjoint_step():
        prior_copies[0].wait_recv()
        for k in range(2):
            remote(edge_send.at[0], edge_got.at[k], pri_send.at[1], pri_recv.at[1 + k], r, other).wait_recv()

        def fill(t, _):
            for k in range(4):
                mine = pl.ds(pl.multiple_of(8 + ch * 32 + 8 * k, 8), 8)
                theirs = pl.ds(pl.multiple_of(8 + other * 32 + 8 * k, 8), 8)
                spread_new[t, mine, :] = wavelet_ref[ch, k, t]
                spread_new[t, theirs, :] = prior_got[k, t]
            spread_new[t, 6:8, :] = jnp.where(r == 0, 0.0, edge_got[0, t])
            spread_new[t, 72:74, :] = jnp.where(r == PEERS - 1, 0.0, edge_got[1, t])
            return 0

        lax.fori_loop(0, 32, fill, 0)

        def close(t, k, filtered):
            image_ref[k, t] = x_ref[k, t] - primal_step * filtered

        def columns(t, carry):
            new = []
            for k in range(8):
                finished, kept = filter_column(
                    lambda p: spread_new[t, 6 + 8 * k + p : 14 + 8 * k + p, :], low_reverse, high_reverse, carry[k]
                )
                close(jnp.maximum(t - 1, 0), k, finished)
                new.append(kept)
            return tuple(new)

        carry = lax.fori_loop(0, 32, columns, ((zero, zero, zero),) * 8)
        for k in range(8):
            close(31, k, carry[k][2])

    lax.fori_loop(0, PRIOR_AFTER, column_piece, 0)
    prior_step()
    lax.fori_loop(PRIOR_AFTER, PIECES, column_piece, 0)

    own_sums[0:1] = jnp.sum(sums[0], axis=0, keepdims=True)
    own_sums[1:2] = jnp.sum(sums[1], axis=0, keepdims=True)
    all_sums[r] = own_sums[...]

    def tell(i, _):
        remote(own_sums, all_sums.at[r], sum_send, sum_recv, lax.rem(r + i, PEERS), ch).start()
        return 0

    lax.fori_loop(1, PEERS, tell, 0)
    adjoint_step()
    every = pl.ds(0, PEERS - 1)
    told = remote(all_sums.at[every], all_sums.at[every], sum_send, sum_recv, after, ch)
    told.wait_recv()
    norms = jnp.sum(all_sums[...], axis=0)
    resid_norm = jnp.sum(norms[0:1], axis=1, keepdims=True)
    data_norm = jnp.sum(norms[1:2], axis=1, keepdims=True)
    shrink = data_step * (1.0 - radius_ref[0] * jnp.sqrt(data_norm) / jnp.sqrt(resid_norm))
    shrink = jnp.broadcast_to(shrink, (8, 128))

    def scale(i, _):
        for v in range(32):
            for part in range(2):
                fourier_ref[part, i, v] = fourier_ref[part, i, v] * shrink
        return 0

    lax.fori_loop(0, 8, scale, 0)

    def back_piece(g, _):
        all_of(sent_back, returned, back_send, back_recv, g).wait_recv()

        def block(a_hi, _):
            rows = []
            for c in range(2):
                for e in range(2):
                    rows.append(returned[pl.ds(chunk_row(g, c, a_hi, e), PEERS, stride=CHUNK), :])
            result = gather(jnp.concatenate(rows), gr_ref)
            for a_lo in range(16):
                row = pl.ds(pl.multiple_of((a_hi * 16 + a_lo) * 32 + g * 8, 8), 8)
                wide[0, row, :] = result[a_lo * 8 : a_lo * 8 + 8, 0:WIDE]
                wide[1, row, :] = result[a_lo * 8 : a_lo * 8 + 8, WIDE:]
            return 0

        lax.fori_loop(0, 4, block, 0)
        return 0

    lax.fori_loop(0, PIECES, back_piece, 0)

    def finish(at, _):
        items = []
        for q in range(RADIX):
            row = pl.ds(at * 256 + q, 8, stride=32)
            items.append(
                c_mul((wide[0, row, :], wide[1, row, :]), tw_ref[0, pl.ds(q, 1), :], -tw_ref[1, pl.ds(q, 1), :])
            )
        done = short_fft(items, 1)
        factor = shrink * primal_step
        for p in range(RADIX):
            image_ref[at, p] = jnp.maximum(image_ref[at, p] - done[p][0] * factor, 0.0)
        return 0

    lax.fori_loop(0, 8, finish, 0)

    for copy in sky_copies + [far_up, far_down] + prior_copies + [told]:
        copy.wait_send()

    def drain(g, _):
        all_of(sent, arrived, send_sem, recv_sem, g).wait_send()
        all_of(sent_back, returned, back_send, back_recv, g).wait_send()
        return 0

    lax.fori_loop(0, PIECES, drain, 0)


def tiles(array):
    lead, n = array.shape[:-2], array.ndim - 2
    array = array.reshape(lead + (array.shape[-2] // 8, 8, 32, 128))
    return array.transpose(tuple(range(n)) + (n, n + 2, n + 1, n + 3))


def untiles(array):
    n = array.ndim - 4
    rows = array.shape[n] * 8
    array = array.transpose(tuple(range(n)) + (n, n + 2, n + 1, n + 3))
    return array.reshape(array.shape[:n] + (rows, SIDE))


def per_device(sky_image, fourier_dual, visibilities, weights, radius, wavelet_dual, reweight):
    forward, backward = dft_matrix(-1.0), dft_matrix(1.0)
    tables = (
        twiddle(-1.0),
        high_low(halves_first(forward.T))[0],
        high_low(halves_first(forward))[0],
        high_low(halves_first(backward.T))[0],
        high_low(halves_first(backward))[0],
    )
    vmem, dma = pltpu.VMEM, pltpu.SemaphoreType.DMA
    in_vmem, in_any = pl.BlockSpec(memory_space=pltpu.VMEM), pl.BlockSpec(memory_space=pl.ANY)
    image, fourier_new, wavelet_new = pl.pallas_call(
        step,
        out_shape=(
            jax.ShapeDtypeStruct((8, 32, 8, 128), F32),
            jax.ShapeDtypeStruct((2, 8, 32, 8, 128), F32),
            jax.ShapeDtypeStruct((2, 4, 32, 8, 128), F32),
        ),
        in_specs=[pl.BlockSpec(memory_space=pltpu.SMEM)] + [in_any] * 6 + [in_vmem] * 5,
        out_specs=(in_vmem,) * 3,
        scratch_shapes=[
            vmem((8, 32, 8, 128), F32), vmem((2, 8, 32, 8, 128), F32), vmem((2, 8, 32, 8, 128), F32),
            vmem((8, 32, 8, 128), F32), vmem((2, 4, 32, 8, 128), F32), vmem((4, 32, 8, 128), F32),
            vmem((4096, 128), F32), vmem((4096, 128), F32), vmem((4096, 128), F32), vmem((4096, 128), F32),
            vmem((16, 128, 256), F32), vmem((2, 2048, 128), F32),
            vmem((2, 8, 128), F32), vmem((2, 128), F32), vmem((PEERS, 2, 128), F32),
            vmem((32, 2, 128), F32), vmem((2, 32, 2, 128), F32),
            vmem((4, 32, 8, 128), F32), vmem((32, 2, 128), F32), vmem((2, 32, 2, 128), F32),
            vmem((2, 32, 48, 128), F32),
            vmem((2, 32, 2, 128), F32), vmem((4, 32, 8, 128), F32), vmem((2, 32, 2, 128), F32),
            vmem((32, 80, 128), F32),
            dma((6,)), dma, dma((PIECES,)), dma((PIECES,)), dma((PIECES,)), dma((PIECES,)),
            dma, dma, dma((4,)), dma((4,)), dma((3,)), dma((3,)),
        ],
        compiler_params=pltpu.CompilerParams(
            collective_id=0, has_side_effects=True, vmem_limit_bytes=60 << 20
        ),
    )(
        radius, tiles(sky_image[0]), tiles(fourier_dual[:, 0]), tiles(visibilities[:, 0]), tiles(weights[0]),
        tiles(wavelet_dual), tiles(reweight), *tables,
    )
    return (untiles(image)[None], untiles(fourier_new)[:, None], untiles(wavelet_new))


def solution(mesh):
    in_specs = (
        P("chan", "row", None),
        P(None, "chan", "row", None),
        P(None, "chan", "row", None),
        P("chan", "row", None),
        P("chan"),
        P(None, ("row", "chan"), None),
        P(("row", "chan"), None),
    )
    out_specs = (
        P("chan", "row", None),
        P(None, "chan", "row", None),
        P(None, ("row", "chan"), None),
    )
    return jax.shard_map(
        per_device, mesh=mesh, in_specs=in_specs, out_specs=out_specs, check_vma=False
    )
```

```python
import math

import jax
import jax.numpy as jnp
import numpy as np
from jax import lax
from jax.experimental import pallas as pl
from jax.experimental.pallas import tpu as pltpu
from jax.sharding import PartitionSpec as P

data_step = 0.8
primal_step = 0.5
low_taps = (0.0625, 0.25, 0.375, 0.25, 0.0625)
high_taps = (-0.1, -0.3, 0.7, -0.2, -0.1)
low_reverse = (0.0625, 0.25, 0.375, 0.25, 0.0625)
high_reverse = (-0.1, -0.2, 0.7, -0.3, -0.1)

F32 = jnp.float32
SIDE = 4096
RADIX = 32
WIDE = 128


def c_add(a, b):
    re = a[0] + b[0]
    if a[1] is None:
        return (re, b[1])
    return (re, a[1] if b[1] is None else a[1] + b[1])


def c_sub(a, b):
    re = a[0] - b[0]
    if a[1] is None:
        return (re, None if b[1] is None else -b[1])
    return (re, a[1] if b[1] is None else a[1] - b[1])


def c_turn(a, k, n, orient):
    re, im = a
    if k == 0:
        return a
    if 4 * k == n:
        if im is None:
            return (None, re if orient > 0 else -re)
        return (-im, re) if orient > 0 else (im, -re)
    cos, sin = math.cos(2 * math.pi * k / n), orient * math.sin(2 * math.pi * k / n)
    if im is None:
        return (re * cos, re * sin)
    if 8 * k == n:
        return ((re - im) * cos, (re + im) * cos) if orient > 0 else ((re + im) * cos, (im - re) * cos)
    if 8 * k == 3 * n:
        c = -cos
        return ((-re - im) * c, (re - im) * c) if orient > 0 else ((im - re) * c, (-re - im) * c)
    return (re * cos - im * sin, re * sin + im * cos)


def short_fft(items, orient):
    n = len(items)
    if n == 1:
        return list(items)
    even = short_fft(items[0::2], orient)
    odd = short_fft(items[1::2], orient)
    low, high = [], []
    for k in range(n // 2):
        if even[k][1] is None and odd[k][1] is None and 4 * k == n:
            low.append((even[k][0], orient * odd[k][0]))
            high.append((even[k][0], -orient * odd[k][0]))
            continue
        turned = c_turn(odd[k], k, n, orient)
        low.append(c_add(even[k], turned))
        high.append(c_sub(even[k], turned))
    return low + high


def dft_matrix(orient):
    idx = np.arange(WIDE)
    angle = 2 * np.pi * ((idx[:, None] * idx[None, :]) % WIDE) / WIDE
    cos, sin = np.cos(angle) / 64.0, orient * np.sin(angle) / 64.0
    return np.block([[cos, sin], [-sin, cos]])


def halves_first(matrix_rows):
    order = np.arange(WIDE).reshape(64, 2).T.reshape(-1)
    return np.concatenate([matrix_rows[:WIDE][order], matrix_rows[WIDE:][order]])


def high_low(matrix):

    bf = np.asarray(matrix, np.float32).astype(jnp.bfloat16)
    low = (np.asarray(matrix) - bf.astype(np.float64)).astype(jnp.bfloat16)
    return (jnp.asarray(np.stack([bf, low])),)


def twiddle(orient):
    angle = 2 * np.pi * (np.arange(RADIX)[:, None] * np.arange(WIDE)[None, :]) / SIDE
    return jnp.asarray(np.stack([np.cos(angle), orient * np.sin(angle)]), jnp.float32)


def split_two(x):
    high = x.astype(jnp.bfloat16)
    return high, (x - high.astype(jnp.float32)).astype(jnp.bfloat16)


def product(dims, a_pair, b_pair):
    def one(a, b):
        return lax.dot_general(a, b, (dims, ((), ())), preferred_element_type=jnp.float32)

    return one(a_pair[0], b_pair[0]) + (one(a_pair[1], b_pair[0]) + one(a_pair[0], b_pair[1]))


def spread(matrix_ref, block):
    return product(((1,), (1,)), (matrix_ref[0], matrix_ref[1]), split_two(block))


def gather(block, matrix_ref):
    return product(((0,), (0,)), split_two(block), (matrix_ref[0], matrix_ref[1]))


def c_mul(a, b_re, b_im):
    return (a[0] * b_re - a[1] * b_im, a[0] * b_im + a[1] * b_re)


MESH = pl.DeviceIdType.MESH
PEERS = 64
CHUNK = 64
PIECE = 16
PIECES = 4
VMEM_MIB = 40


def chunk_row(g, c, a_hi, e):
    return g * PIECE + (a_hi // 2) * 8 + c * 4 + (a_hi % 2) * 2 + e


def step(
    radius_ref, x_hbm, prior_hbm, limit_hbm, dual_hbm, vis_hbm, weight_hbm, tw_hbm, rows_hbm, columns_hbm,
    image_ref, fourier_ref, wavelet_ref,
    x_ref, dual_ref, vis_ref, weight_ref, prior_ref, limit_ref, tw_ref, rows_ref, columns_ref,
    sent, arrived, sent_back, returned, held, facet_held, facet_sent, wide, sums, own_sums, all_sums,
    near_send, far_send, sky_got, near_got, far_got, grown, edge_send, prior_got, edge_got, spread_new,
    load_sem, own_sem, send_sem, recv_sem, back_send, back_recv, sum_send, sum_recv, sky_send, sky_recv, pri_send, pri_recv,
):
    r, ch = lax.axis_index("row"), lax.axis_index("chan")
    other = 1 - ch
    after, before = lax.rem(r + 1, PEERS), lax.rem(r + PEERS - 1, PEERS)

    loads = [
        pltpu.make_async_copy(src, dst, load_sem.at[i])
        for i, (src, dst) in enumerate(
            (
                (x_hbm, x_ref), (tw_hbm, tw_ref), (rows_hbm, rows_ref), (columns_hbm, columns_ref),
                (prior_hbm, prior_ref), (limit_hbm, limit_ref),
                (dual_hbm, dual_ref), (vis_hbm, vis_ref), (weight_hbm, weight_ref),
            )
        )
    ]
    for load in loads:
        load.start()

    barrier = pltpu.get_barrier_semaphore()

    def greet_other(i, _):
        pl.semaphore_signal(barrier, inc=1, device_id=(lax.rem(r + i, PEERS), other), device_id_type=MESH)
        return 0

    def greet(i, _):
        pl.semaphore_signal(barrier, inc=1, device_id=(lax.rem(r + i, PEERS), ch), device_id_type=MESH)
        return 0

    lax.fori_loop(1, PEERS, greet, 0)
    lax.fori_loop(0, PEERS, greet_other, 0)

    def remote(src, dst, send, recv, row, chan):
        return pltpu.make_async_remote_copy(
            src_ref=src, dst_ref=dst, send_sem=send, recv_sem=recv, device_id=(row, chan), device_id_type=MESH
        )

    loads[0].wait()
    loads[1].wait()

    def turn_rows(done, into, blocks, at):
        a_hi, a_mid = at // 2, at % 2
        for q in range(RADIX):
            value = done[q]
            if value[1] is None:
                re = value[0] * tw_ref[0, pl.ds(q, 1), :]
                im = value[0] * tw_ref[1, pl.ds(q, 1), :]
            else:
                re, im = c_mul(value, tw_ref[0, pl.ds(q, 1), :], tw_ref[1, pl.ds(q, 1), :])
            row = pl.ds(pl.multiple_of((q % 8) * 16 + a_mid * 8, 8), 8)
            into[(q // 8) * blocks + a_hi, row, 0:WIDE] = re
            into[(q // 8) * blocks + a_hi, row, WIDE:] = im

    side, z, low = (r // 8) % 2, r // 16, r % 8

    def peer(i, its_side):
        return lax.rem(z + i // 8, 4) * 16 + its_side * 8 + lax.rem(low + i % 8, 8)

    def row_short(at, _):
        items = [(x_ref[at, p], None) for p in range(RADIX)]
        done = short_fft(items, -1)
        turn_rows(done, held, 4, at)
        return 0

    lax.fori_loop(0, 8, row_short, 0)

    first_here = ch == 0

    def edges(t, _):
        low, high = x_ref[4, t][0:2], x_ref[3, t][6:8]
        near_send[t] = jnp.where(first_here, high, low)
        far_send[0, t] = x_ref[7, t][6:8]
        far_send[1, t] = x_ref[0, t][0:2]
        return 0

    lax.fori_loop(0, 32, edges, 0)
    pl.semaphore_wait(barrier, 2 * PEERS - 1)

    half = pl.ds(pl.multiple_of(other * 4, 4), 4)
    sky_copies = [
        remote(x_ref.at[half], sky_got, sky_send.at[0], sky_recv.at[0], r, other),
        remote(near_send, near_got, sky_send.at[1], sky_recv.at[1], r, other),
    ]
    for copy in sky_copies:
        copy.start()
    far_up = remote(far_send.at[0], far_got.at[ch], sky_send.at[2], sky_recv.at[2 + ch], after, 0)
    far_down = remote(far_send.at[1], far_got.at[ch], sky_send.at[3], sky_recv.at[2 + ch], before, 1)
    far_up.start()
    far_down.start()

    loads[2].wait()
    def back_copies(g, its_side, first):
        def one(i, _):
            d = peer(i, its_side)
            take = pl.ds(pl.multiple_of(d * CHUNK + g * PIECE, PIECE), PIECE)
            give = pl.ds(pl.multiple_of(r * CHUNK + g * PIECE, PIECE), PIECE)
            remote(sent_back.at[take], returned.at[give], back_send.at[g], back_recv.at[g], d, ch).start()
            return 0

        lax.fori_loop(first, PEERS // 2, one, 0)

    def all_of(src, dst, send, recv, g):
        rows = pl.ds(0, (PEERS - 1) * PIECE)
        return remote(src.at[rows], dst.at[rows], send.at[g], recv.at[g], after, ch)

    def row_piece(g, _):
        def block(a_hi, _):
            result = spread(rows_ref, held[g * 4 + a_hi])
            for c in range(2):
                for e in range(2):
                    for d in range(0, 64, 8):
                        m = c * 128 + e * 64 + d
                        sent[pl.ds(d * CHUNK + chunk_row(g, c, a_hi, e), 8, stride=CHUNK), :] = result[m : m + 8]
            return 0

        lax.fori_loop(0, 4, block, 0, unroll=True)

        def one(i, _):
            d = peer(i, side)
            take = pl.ds(pl.multiple_of(d * CHUNK + g * PIECE, PIECE), PIECE)
            give = pl.ds(pl.multiple_of(r * CHUNK + g * PIECE, PIECE), PIECE)
            remote(sent.at[take], arrived.at[give], send_sem.at[g], recv_sem.at[g], d, ch).start()
            return 0

        lax.fori_loop(1, PEERS // 2, one, 0)
        mine = pl.ds(pl.multiple_of(r * CHUNK + g * PIECE, PIECE), PIECE)
        own = pltpu.make_async_copy(sent.at[mine], arrived.at[mine], own_sem)
        own.start()
        own.wait()
        return 0

    lax.fori_loop(0, PIECES, row_piece, 0)

    for copy in sky_copies:
        copy.wait_recv()

    def facet_short(at, _):
        done = short_fft([(sky_got[at, p], None) for p in range(RADIX)], -1)
        turn_rows(done, facet_held, 2, at)
        return 0

    lax.fori_loop(0, 4, facet_short, 0)

    def facet_piece(g, _):
        def own_half(i, _):
            d = peer(i, 1 - side)
            take = pl.ds(pl.multiple_of(d * CHUNK + g * PIECE + ch * 8, 8), 8)
            give = pl.ds(pl.multiple_of(r * CHUNK + g * PIECE + ch * 8, 8), 8)
            remote(sent.at[take], arrived.at[give], send_sem.at[g], recv_sem.at[g], d, ch).start()
            return 0

        lax.fori_loop(0, PEERS // 2, own_half, 0)

        def block(l_hi, _):
            result = spread(rows_ref, facet_held[g * 2 + l_hi])
            for c in range(2):
                for e in range(2):
                    for d in range(0, 64, 8):
                        m = c * 128 + e * 64 + d
                        start = d * 32 + g * 8 + c * 4 + l_hi * 2 + e
                        facet_sent[pl.ds(start, 8, stride=32), :] = result[m : m + 8]
            return 0

        lax.fori_loop(0, 2, block, 0, unroll=True)

        def other_half(i, _):
            d = peer(i, 1 - side)
            take = pl.ds(pl.multiple_of(d * 32 + g * 8, 8), 8)
            give = pl.ds(pl.multiple_of(r * CHUNK + g * PIECE + ch * 8, 8), 8)
            remote(facet_sent.at[take], arrived.at[give], send_sem.at[g], recv_sem.at[g], d, other).start()
            return 0

        lax.fori_loop(0, PEERS // 2, other_half, 0)
        return 0

    lax.fori_loop(0, PIECES, facet_piece, 0)

    for load in loads[3:4] + loads[6:]:
        load.wait()
    sums[...] = jnp.zeros_like(sums)

    def column_piece(g, _):
        def block(i, _):
            l_hi, e = i // 2, i % 2
            rows = []
            for c in range(2):
                for jh in range(2):
                    rows.append(arrived[pl.ds(chunk_row(g, c, jh * 2 + l_hi, e), PEERS, stride=CHUNK), :])
            result = gather(jnp.concatenate(rows), columns_ref)
            for q_lo in range(8):
                row = pl.ds(pl.multiple_of(((e * 4 + g) * 8 + q_lo) * 32 + l_hi * 16, 16), 16)
                wide[0, row, :] = result[q_lo * 16 : q_lo * 16 + 16, 0:WIDE]
                wide[1, row, :] = result[q_lo * 16 : q_lo * 16 + 16, WIDE:]
            return 0

        lax.fori_loop(0, 4, block, 0, unroll=True)

        def short(e, _):
            q_hi = e * 4 + g
            items = []
            for l in range(RADIX):
                row = pl.ds(q_hi * 256 + l, 8, stride=32)
                items.append(
                    c_mul((wide[0, row, :], wide[1, row, :]), tw_ref[0, pl.ds(l, 1), :], tw_ref[1, pl.ds(l, 1), :])
                )
            freq = short_fft(items, -1)
            total, total_vis = sums[0], sums[1]
            items = []
            for v in range(RADIX):
                weight = weight_ref[q_hi, v]
                vis_re, vis_im = vis_ref[0, q_hi, v], vis_ref[1, q_hi, v]
                re = dual_ref[0, q_hi, v] * (1.0 / data_step) + weight * freq[v][0] - vis_re
                im = dual_ref[1, q_hi, v] * (1.0 / data_step) + weight * freq[v][1] - vis_im
                total = total + (re * re + im * im)
                total_vis = total_vis + (vis_re * vis_re + vis_im * vis_im)
                fourier_ref[0, q_hi, v] = re
                fourier_ref[1, q_hi, v] = im
                items.append((weight * re, weight * im))
            sums[0] = total
            sums[1] = total_vis
            done = short_fft(items, 1)
            for l in range(RADIX):
                re, im = c_mul(done[l], tw_ref[0, pl.ds(l, 1), :], -tw_ref[1, pl.ds(l, 1), :])
                row = pl.ds((l % 16) * 8, 8)
                held[(l // 16) * 8 + q_hi, row, 0:WIDE] = re
                held[(l // 16) * 8 + q_hi, row, WIDE:] = im
            return 0

        lax.fori_loop(0, 2, short, 0)

        def block_back(i, _):
            l_hi, e = i // 2, i % 2
            result = spread(columns_ref, held[l_hi * 8 + e * 4 + g])
            for c in range(2):
                for jh in range(2):
                    for s in range(0, 64, 8):
                        m = c * 128 + jh * 64 + s
                        start = s * CHUNK + chunk_row(g, c, jh * 2 + l_hi, e)
                        sent_back[pl.ds(start, 8, stride=CHUNK), :] = result[m : m + 8]
            return 0

        lax.fori_loop(0, 4, block_back, 0, unroll=True)
        back_copies(g, side, 1)
        mine = pl.ds(pl.multiple_of(r * CHUNK + g * PIECE, PIECE), PIECE)
        own = pltpu.make_async_copy(sent_back.at[mine], returned.at[mine], own_sem)
        own.start()
        own.wait()
        return 0

    def later_piece(g, _):
        all_of(sent, arrived, send_sem, recv_sem, g).wait_recv()
        column_piece(g, 0)
        back_copies(g - 1, 1 - side, 0)
        return 0

    lane = lax.broadcasted_iota(jnp.int32, (8, 128), 1)

    def filter_column(load, low_set, high_set, carry):
        taps = [load(p) for p in range(5)]
        low = taps[0] * low_set[0]
        high = taps[0] * high_set[0]
        for p in range(1, 5):
            low = low + taps[p] * low_set[p]
            high = high + taps[p] * high_set[p]
        return finish_column(low, high, low_set, high_set, carry)

    def finish_column(low, high, low_set, high_set, carry):
        old0, old1, unfinished = carry
        terms = [high * low_set[p] + low * high_set[p] for p in range(5)]
        new0 = pltpu.roll(terms[0], 2, 1)
        new1 = pltpu.roll(terms[1], 1, 1)
        new3 = pltpu.roll(terms[3], 127, 1)
        new4 = pltpu.roll(terms[4], 126, 1)
        finished = unfinished + jnp.where(lane >= 127, new3, 0.0) + jnp.where(lane >= 126, new4, 0.0)
        started = (
            terms[2]
            + (jnp.where(lane >= 2, new0, old0) + jnp.where(lane >= 1, new1, old1))
            + (jnp.where(lane < 127, new3, 0.0) + jnp.where(lane < 126, new4, 0.0))
        )
        return finished, (new0, new1, started)

    zero = jnp.zeros((8, 128), F32)
    prior_copies = [
        remote(wavelet_ref.at[other], prior_got, pri_send.at[0], pri_recv.at[0], r, other)
    ] + [
        remote(
            edge_send.at[c], edge_got.at[1 - ch], pri_send.at[1 + c], pri_recv.at[2 - ch],
            lax.rem(r + PEERS - 1 + 2 * ch, PEERS), c,
        )
        for c in range(2)
    ]

    def prior_step():
        for load in loads[4:6]:
            load.wait()
        for k in range(2):
            remote(far_send.at[0], far_got.at[k], sky_send.at[2], sky_recv.at[2 + k], r, other).wait_recv()
        no_far = jnp.logical_or(
            jnp.logical_and(ch == 0, r == 0), jnp.logical_and(ch == 1, r == PEERS - 1)
        )

        def grow(t, _):
            for k in range(4):
                grown[ch, t, 8 + 8 * k : 16 + 8 * k, :] = x_ref[ch * 4 + k, t]
                grown[other, t, 8 + 8 * k : 16 + 8 * k, :] = sky_got[k, t]
            near_own = jnp.where(first_here, x_ref[4, t][0:2], x_ref[3, t][6:8])
            near_other = near_got[t]
            far_own = jnp.where(no_far, 0.0, far_got[ch, t])
            far_other = jnp.where(no_far, 0.0, far_got[other, t])
            grown[ch, t, 6:8, :] = jnp.where(first_here, far_own, near_own)
            grown[ch, t, 40:42, :] = jnp.where(first_here, near_own, far_own)
            grown[other, t, 6:8, :] = jnp.where(first_here, far_other, near_other)
            grown[other, t, 40:42, :] = jnp.where(first_here, near_other, far_other)
            return 0

        lax.fori_loop(0, 32, grow, 0)

        def close(t, filtered):
            for k in range(4):
                s0 = prior_ref[0, k, t] + filtered[0][k]
                s1 = prior_ref[1, k, t] + filtered[1][k]
                limit = limit_ref[k, t]
                scale = limit / jnp.maximum(jnp.sqrt(s0 * s0 + s1 * s1), limit)
                wavelet_ref[0, k, t] = s0 * scale
                wavelet_ref[1, k, t] = s1 * scale

        def columns(t, carry):
            filtered, new = [[], []], []
            for c in range(2):
                for k in range(4):
                    finished, kept = filter_column(
                        lambda p: grown[c, t, 6 + 8 * k + p : 14 + 8 * k + p, :], low_taps, high_taps, carry[c * 4 + k]
                    )
                    filtered[c].append(finished)
                    new.append(kept)
            close(jnp.maximum(t - 1, 0), filtered)
            return tuple(new)

        carry = lax.fori_loop(0, 32, columns, ((zero, zero, zero),) * 8)
        close(31, [[carry[c * 4 + k][2] for k in range(4)] for c in range(2)])

        def edge(t, _):
            for c in range(2):
                edge_send[c, t] = jnp.where(
                    first_here, wavelet_ref[c, 0, t][0:2], wavelet_ref[c, 3, t][6:8]
                )
            return 0

        lax.fori_loop(0, 32, edge, 0)


    def adjoint_step():
        prior_copies[0].wait_recv()
        for k in range(2):
            remote(edge_send.at[0], edge_got.at[k], pri_send.at[1], pri_recv.at[1 + k], r, other).wait_recv()

        def fill(t, _):
            for k in range(4):
                mine = pl.ds(pl.multiple_of(8 + ch * 32 + 8 * k, 8), 8)
                theirs = pl.ds(pl.multiple_of(8 + other * 32 + 8 * k, 8), 8)
                spread_new[t, mine, :] = wavelet_ref[ch, k, t]
                spread_new[t, theirs, :] = prior_got[k, t]
            spread_new[t, 6:8, :] = jnp.where(r == 0, 0.0, edge_got[0, t])
            spread_new[t, 72:74, :] = jnp.where(r == PEERS - 1, 0.0, edge_got[1, t])
            return 0

        lax.fori_loop(0, 32, fill, 0)

        def close(t, k, filtered):
            image_ref[k, t] = x_ref[k, t] - primal_step * filtered

        def columns(t, carry):
            new = []
            for k in range(8):
                finished, kept = filter_column(
                    lambda p: spread_new[t, 6 + 8 * k + p : 14 + 8 * k + p, :], low_reverse, high_reverse, carry[k]
                )
                close(jnp.maximum(t - 1, 0), k, finished)
                new.append(kept)
            return tuple(new)

        carry = lax.fori_loop(0, 32, columns, ((zero, zero, zero),) * 8)
        for k in range(8):
            close(31, k, carry[k][2])

    prior_step()
    all_of(sent, arrived, send_sem, recv_sem, 0).wait_recv()
    for copy in prior_copies:
        copy.start()
    column_piece(0, 0)
    lax.fori_loop(1, PIECES, later_piece, 0)
    back_copies(PIECES - 1, 1 - side, 0)

    own_sums[0:1] = jnp.sum(sums[0], axis=0, keepdims=True)
    own_sums[1:2] = jnp.sum(sums[1], axis=0, keepdims=True)
    all_sums[r] = own_sums[...]

    def tell(i, _):
        remote(own_sums, all_sums.at[r], sum_send, sum_recv, lax.rem(r + i, PEERS), ch).start()
        return 0

    lax.fori_loop(1, PEERS, tell, 0)
    adjoint_step()
    every = pl.ds(0, PEERS - 1)
    told = remote(all_sums.at[every], all_sums.at[every], sum_send, sum_recv, after, ch)
    told.wait_recv()
    norms = jnp.sum(all_sums[...], axis=0)
    resid_norm = jnp.sum(norms[0:1], axis=1, keepdims=True)
    data_norm = jnp.sum(norms[1:2], axis=1, keepdims=True)
    shrink = data_step * (1.0 - radius_ref[0] * jnp.sqrt(data_norm) / jnp.sqrt(resid_norm))
    shrink = jnp.broadcast_to(shrink, (8, 128))

    def scale(i, _):
        for v in range(32):
            for part in range(2):
                fourier_ref[part, i, v] = fourier_ref[part, i, v] * shrink
        return 0

    lax.fori_loop(0, 8, scale, 0)

    def back_piece(g, _):
        all_of(sent_back, returned, back_send, back_recv, g).wait_recv()

        def block(a_hi, _):
            rows = []
            for c in range(2):
                for e in range(2):
                    rows.append(returned[pl.ds(chunk_row(g, c, a_hi, e), PEERS, stride=CHUNK), :])
            result = gather(jnp.concatenate(rows), rows_ref)
            for a_lo in range(16):
                row = pl.ds(pl.multiple_of((a_hi * 16 + a_lo) * 32 + g * 8, 8), 8)
                wide[0, row, :] = result[a_lo * 8 : a_lo * 8 + 8, 0:WIDE]
                wide[1, row, :] = result[a_lo * 8 : a_lo * 8 + 8, WIDE:]
            return 0

        lax.fori_loop(0, 4, block, 0, unroll=True)
        return 0

    lax.fori_loop(0, PIECES, back_piece, 0)

    def finish(at, _):
        items = []
        for q in range(RADIX):
            row = pl.ds(at * 256 + q, 8, stride=32)
            items.append(
                c_mul((wide[0, row, :], wide[1, row, :]), tw_ref[0, pl.ds(q, 1), :], -tw_ref[1, pl.ds(q, 1), :])
            )
        done = short_fft(items, 1)
        factor = shrink * primal_step
        for p in range(RADIX):
            image_ref[at, p] = jnp.maximum(image_ref[at, p] - done[p][0] * factor, 0.0)
        return 0

    lax.fori_loop(0, 8, finish, 0)

    for copy in sky_copies + [far_up, far_down] + prior_copies + [told]:
        copy.wait_send()

    def drain(g, _):
        all_of(sent, arrived, send_sem, recv_sem, g).wait_send()
        all_of(sent_back, returned, back_send, back_recv, g).wait_send()
        return 0

    lax.fori_loop(0, PIECES, drain, 0)


def store(a, b, c, out_a, out_b, out_c, sem):
    copies = [
        pltpu.make_async_copy(src, dst, sem.at[i]) for i, (src, dst) in enumerate(((a, out_a), (b, out_b), (c, out_c)))
    ]
    for copy in copies:
        copy.start()
    for copy in copies:
        copy.wait()


def tiles(array):
    lead, n = array.shape[:-2], array.ndim - 2
    array = array.reshape(lead + (array.shape[-2] // 8, 8, 32, 128))
    return array.transpose(tuple(range(n)) + (n, n + 2, n + 1, n + 3))


def untiles(array):
    n = array.ndim - 4
    rows = array.shape[n] * 8
    array = array.transpose(tuple(range(n)) + (n, n + 2, n + 1, n + 3))
    return array.reshape(array.shape[:n] + (rows, SIDE))


def per_device(sky_image, fourier_dual, visibilities, weights, radius, wavelet_dual, reweight):
    forward, backward = dft_matrix(-1.0), dft_matrix(1.0)
    tables = (
        twiddle(-1.0),
        high_low(halves_first(backward))[0],
        high_low(halves_first(forward))[0],
    )
    vmem, dma = pltpu.VMEM, pltpu.SemaphoreType.DMA
    in_vmem, in_hbm = pl.BlockSpec(memory_space=pltpu.VMEM), pl.BlockSpec(memory_space=pltpu.HBM)
    image, fourier_new, wavelet_new = pl.pallas_call(
        step,
        out_shape=(
            jax.ShapeDtypeStruct((8, 32, 8, 128), F32),
            jax.ShapeDtypeStruct((2, 8, 32, 8, 128), F32),
            jax.ShapeDtypeStruct((2, 4, 32, 8, 128), F32),
        ),
        in_specs=[pl.BlockSpec(memory_space=pltpu.SMEM)] + [in_hbm] * 9,
        out_specs=(in_vmem,) * 3,
        scratch_shapes=[
            vmem((8, 32, 8, 128), F32), vmem((2, 8, 32, 8, 128), F32), vmem((2, 8, 32, 8, 128), F32),
            vmem((8, 32, 8, 128), F32), vmem((2, 4, 32, 8, 128), F32), vmem((4, 32, 8, 128), F32),
            vmem((2, RADIX, WIDE), F32), vmem((2, 256, 256), jnp.bfloat16), vmem((2, 256, 256), jnp.bfloat16),
            vmem((4096, 128), F32), vmem((4096, 128), F32), vmem((4096, 128), F32), vmem((4096, 128), F32),
            vmem((16, 128, 256), F32), vmem((8, 128, 256), F32), vmem((2048, 128), F32), vmem((2, 2048, 128), F32),
            vmem((2, 8, 128), F32), vmem((2, 128), F32), vmem((PEERS, 2, 128), F32),
            vmem((32, 2, 128), F32), vmem((2, 32, 2, 128), F32),
            vmem((4, 32, 8, 128), F32), vmem((32, 2, 128), F32), vmem((2, 32, 2, 128), F32),
            vmem((2, 32, 48, 128), F32),
            vmem((2, 32, 2, 128), F32), vmem((4, 32, 8, 128), F32), vmem((2, 32, 2, 128), F32),
            vmem((32, 80, 128), F32),
            dma((9,)), dma, dma((PIECES,)), dma((PIECES,)), dma((PIECES,)), dma((PIECES,)),
            dma, dma, dma((4,)), dma((4,)), dma((3,)), dma((3,)),
        ],
        compiler_params=pltpu.CompilerParams(
            collective_id=0, has_side_effects=True, vmem_limit_bytes=VMEM_MIB << 20
        ),
    )(
        radius, *(pltpu.with_memory_space_constraint(v, pltpu.HBM) for v in (
            *map(tiles, (sky_image[0], wavelet_dual, reweight, fourier_dual[:, 0], visibilities[:, 0], weights[0])), *tables)),
    )
    results = (image, fourier_new, wavelet_new)
    image, fourier_new, wavelet_new = pl.pallas_call(
        store,
        out_shape=tuple(jax.ShapeDtypeStruct(v.shape, F32) for v in results),
        in_specs=[in_vmem] * 3,
        out_specs=(in_hbm,) * 3,
        scratch_shapes=[dma((3,))],
        compiler_params=pltpu.CompilerParams(vmem_limit_bytes=4 << 20),
    )(*results)
    return (untiles(image)[None], untiles(fourier_new)[:, None], untiles(wavelet_new))


def solution(mesh):
    in_specs = (
        P("chan", "row", None),
        P(None, "chan", "row", None),
        P(None, "chan", "row", None),
        P("chan", "row", None),
        P("chan"),
        P(None, ("row", "chan"), None),
        P(("row", "chan"), None),
    )
    out_specs = (
        P("chan", "row", None),
        P(None, "chan", "row", None),
        P(None, ("row", "chan"), None),
    )
    return jax.shard_map(
        per_device, mesh=mesh, in_specs=in_specs, out_specs=out_specs, check_vma=False
    )
```

```python
import math

import jax
import jax.numpy as jnp
import numpy as np
from jax import lax
from jax.experimental import pallas as pl
from jax.experimental.pallas import tpu as pltpu
from jax.sharding import PartitionSpec as P

data_step = 0.8
primal_step = 0.5
low_taps = (0.0625, 0.25, 0.375, 0.25, 0.0625)
high_taps = (-0.1, -0.3, 0.7, -0.2, -0.1)
low_reverse = (0.0625, 0.25, 0.375, 0.25, 0.0625)
high_reverse = (-0.1, -0.2, 0.7, -0.3, -0.1)

F32 = jnp.float32
SIDE = 4096
RADIX = 32
WIDE = 128


def c_add(a, b):
    re = a[0] + b[0]
    if a[1] is None:
        return (re, b[1])
    return (re, a[1] if b[1] is None else a[1] + b[1])


def c_sub(a, b):
    re = a[0] - b[0]
    if a[1] is None:
        return (re, None if b[1] is None else -b[1])
    return (re, a[1] if b[1] is None else a[1] - b[1])


def c_turn(a, k, n, orient):
    re, im = a
    if k == 0:
        return a
    if 4 * k == n:
        if im is None:
            return (None, re if orient > 0 else -re)
        return (-im, re) if orient > 0 else (im, -re)
    cos, sin = math.cos(2 * math.pi * k / n), orient * math.sin(2 * math.pi * k / n)
    if im is None:
        return (re * cos, re * sin)
    if 8 * k == n:
        return ((re - im) * cos, (re + im) * cos) if orient > 0 else ((re + im) * cos, (im - re) * cos)
    if 8 * k == 3 * n:
        c = -cos
        return ((-re - im) * c, (re - im) * c) if orient > 0 else ((im - re) * c, (-re - im) * c)
    return (re * cos - im * sin, re * sin + im * cos)


def short_fft(items, orient):
    n = len(items)
    if n == 1:
        return list(items)
    even = short_fft(items[0::2], orient)
    odd = short_fft(items[1::2], orient)
    low, high = [], []
    for k in range(n // 2):
        if even[k][1] is None and odd[k][1] is None and 4 * k == n:
            low.append((even[k][0], orient * odd[k][0]))
            high.append((even[k][0], -orient * odd[k][0]))
            continue
        turned = c_turn(odd[k], k, n, orient)
        low.append(c_add(even[k], turned))
        high.append(c_sub(even[k], turned))
    return low + high


def dft_matrix(orient):
    idx = np.arange(WIDE)
    angle = 2 * np.pi * ((idx[:, None] * idx[None, :]) % WIDE) / WIDE
    cos, sin = np.cos(angle) / 64.0, orient * np.sin(angle) / 64.0
    return np.block([[cos, sin], [-sin, cos]])


def halves_first(matrix_rows):
    order = np.arange(WIDE).reshape(64, 2).T.reshape(-1)
    return np.concatenate([matrix_rows[:WIDE][order], matrix_rows[WIDE:][order]])


def high_low(matrix):

    bf = np.asarray(matrix, np.float32).astype(jnp.bfloat16)
    low = (np.asarray(matrix) - bf.astype(np.float64)).astype(jnp.bfloat16)
    return (jnp.asarray(np.stack([bf, low])),)


def twiddle(orient):
    angle = 2 * np.pi * (np.arange(RADIX)[:, None] * np.arange(WIDE)[None, :]) / SIDE
    return jnp.asarray(np.stack([np.cos(angle), orient * np.sin(angle)]), jnp.float32)


def split_two(x):
    high = x.astype(jnp.bfloat16)
    return high, (x - high.astype(jnp.float32)).astype(jnp.bfloat16)


def product(dims, a_pair, b_pair):
    def one(a, b):
        return lax.dot_general(a, b, (dims, ((), ())), preferred_element_type=jnp.float32)

    return one(a_pair[0], b_pair[0]) + (one(a_pair[1], b_pair[0]) + one(a_pair[0], b_pair[1]))


def spread(matrix_ref, block):
    return product(((1,), (1,)), (matrix_ref[0], matrix_ref[1]), split_two(block))


def gather(block, matrix_ref):
    return product(((0,), (0,)), split_two(block), (matrix_ref[0], matrix_ref[1]))


def c_mul(a, b_re, b_im):
    return (a[0] * b_re - a[1] * b_im, a[0] * b_im + a[1] * b_re)


MESH = pl.DeviceIdType.MESH
PEERS = 64
CHUNK = 64
PIECE = 16
PIECES = 4
VMEM_MIB = 40


def chunk_row(g, c, a_hi, e):
    return g * PIECE + (a_hi // 2) * 8 + c * 4 + (a_hi % 2) * 2 + e


def step(
    radius_ref, x_hbm, prior_hbm, limit_hbm, dual_hbm, vis_hbm, weight_hbm, tw_hbm, rows_hbm, columns_hbm,
    image_ref, fourier_ref, wavelet_ref, wide, factor_ref,
    x_ref, dual_ref, vis_ref, weight_ref, prior_ref, limit_ref, tw_ref, rows_ref, columns_ref,
    sent, arrived, sent_back, returned, held, facet_held, facet_sent, sums, own_sums, all_sums,
    near_send, far_send, sky_got, near_got, far_got, grown, edge_send, prior_got, edge_got, spread_new,
    load_sem, own_sem, send_sem, recv_sem, back_send, back_recv, sum_send, sum_recv, sky_send, sky_recv, pri_send, pri_recv,
):
    r, ch = lax.axis_index("row"), lax.axis_index("chan")
    other = 1 - ch
    after, before = lax.rem(r + 1, PEERS), lax.rem(r + PEERS - 1, PEERS)

    side, z, low = (r // 8) % 2, r // 16, r % 8

    def peer(i, its_side):
        return lax.rem(z + i // 8, 4) * 16 + its_side * 8 + lax.rem(low + i % 8, 8)

    barrier = pltpu.get_barrier_semaphore()

    def greet(i, _):
        pl.semaphore_signal(barrier, inc=1, device_id=(lax.rem(r + i, PEERS), ch), device_id_type=MESH)
        return 0

    def greet_other(i, _):
        pl.semaphore_signal(barrier, inc=1, device_id=(peer(i, 1 - side), other), device_id_type=MESH)
        return 0

    lax.fori_loop(0, PEERS // 2, greet_other, 0)
    lax.fori_loop(1, PEERS, greet, 0)
    for row in (after, before, r):
        pl.semaphore_signal(barrier, inc=1, device_id=(row, other), device_id_type=MESH)

    loads = [
        pltpu.make_async_copy(src, dst, load_sem.at[i])
        for i, (src, dst) in enumerate(
            (
                (x_hbm, x_ref), (tw_hbm, tw_ref), (rows_hbm, rows_ref), (columns_hbm, columns_ref),
                (prior_hbm, prior_ref), (limit_hbm, limit_ref),
                (dual_hbm, dual_ref), (vis_hbm, vis_ref), (weight_hbm, weight_ref),
            )
        )
    ]
    for load in loads:
        load.start()

    def remote(src, dst, send, recv, row, chan):
        return pltpu.make_async_remote_copy(
            src_ref=src, dst_ref=dst, send_sem=send, recv_sem=recv, device_id=(row, chan), device_id_type=MESH
        )

    loads[0].wait()
    loads[1].wait()

    def turn_rows(done, into, blocks, at):
        a_hi, a_mid = at // 2, at % 2
        for q in range(RADIX):
            value = done[q]
            if value[1] is None:
                re = value[0] * tw_ref[0, pl.ds(q, 1), :]
                im = value[0] * tw_ref[1, pl.ds(q, 1), :]
            else:
                re, im = c_mul(value, tw_ref[0, pl.ds(q, 1), :], tw_ref[1, pl.ds(q, 1), :])
            row = pl.ds(pl.multiple_of((q % 8) * 16 + a_mid * 8, 8), 8)
            into[(q // 8) * blocks + a_hi, row, 0:WIDE] = re
            into[(q // 8) * blocks + a_hi, row, WIDE:] = im

    def row_short(at, _):
        items = [(x_ref[at, p], None) for p in range(RADIX)]
        done = short_fft(items, -1)
        turn_rows(done, held, 4, at)
        return 0

    lax.fori_loop(0, 8, row_short, 0)

    first_here = ch == 0

    def edges(t, _):
        low, high = x_ref[4, t][0:2], x_ref[3, t][6:8]
        near_send[t] = jnp.where(first_here, high, low)
        far_send[0, t] = x_ref[7, t][6:8]
        far_send[1, t] = x_ref[0, t][0:2]
        return 0

    lax.fori_loop(0, 32, edges, 0)
    pl.semaphore_wait(barrier, PEERS - 1 + PEERS // 2 + 3)

    half = pl.ds(pl.multiple_of(other * 4, 4), 4)
    sky_copies = [
        remote(x_ref.at[half], sky_got, sky_send.at[0], sky_recv.at[0], r, other),
        remote(near_send, near_got, sky_send.at[1], sky_recv.at[1], r, other),
    ]
    for copy in sky_copies:
        copy.start()
    far_up = remote(far_send.at[0], far_got.at[ch], sky_send.at[2], sky_recv.at[2 + ch], after, 0)
    far_down = remote(far_send.at[1], far_got.at[ch], sky_send.at[3], sky_recv.at[2 + ch], before, 1)
    far_up.start()
    far_down.start()

    loads[2].wait()
    def back_copies(g, its_side, first):
        def one(i, _):
            d = peer(i, its_side)
            take = pl.ds(pl.multiple_of(d * CHUNK + g * PIECE, PIECE), PIECE)
            give = pl.ds(pl.multiple_of(r * CHUNK + g * PIECE, PIECE), PIECE)
            remote(sent_back.at[take], returned.at[give], back_send.at[g], back_recv.at[g], d, ch).start()
            return 0

        lax.fori_loop(first, PEERS // 2, one, 0)

    def all_of(src, dst, send, recv, g):
        rows = pl.ds(0, (PEERS - 1) * PIECE)
        return remote(src.at[rows], dst.at[rows], send.at[g], recv.at[g], after, ch)

    def row_piece(g, _):
        def block(a_hi, _):
            result = spread(rows_ref, held[g * 4 + a_hi])
            for c in range(2):
                for e in range(2):
                    for d in range(0, 64, 8):
                        m = c * 128 + e * 64 + d
                        sent[pl.ds(d * CHUNK + chunk_row(g, c, a_hi, e), 8, stride=CHUNK), :] = result[m : m + 8]
            return 0

        lax.fori_loop(0, 4, block, 0, unroll=True)

        def one(i, _):
            d = peer(i, side)
            take = pl.ds(pl.multiple_of(d * CHUNK + g * PIECE, PIECE), PIECE)
            give = pl.ds(pl.multiple_of(r * CHUNK + g * PIECE, PIECE), PIECE)
            remote(sent.at[take], arrived.at[give], send_sem.at[g], recv_sem.at[g], d, ch).start()
            return 0

        lax.fori_loop(1, PEERS // 2, one, 0)
        mine = pl.ds(pl.multiple_of(r * CHUNK + g * PIECE, PIECE), PIECE)
        own = pltpu.make_async_copy(sent.at[mine], arrived.at[mine], own_sem)
        own.start()
        own.wait()
        return 0

    lax.fori_loop(0, PIECES, row_piece, 0)

    for copy in sky_copies:
        copy.wait_recv()

    def facet_short(at, _):
        done = short_fft([(sky_got[at, p], None) for p in range(RADIX)], -1)
        turn_rows(done, facet_held, 2, at)
        return 0

    lax.fori_loop(0, 4, facet_short, 0)

    def facet_piece(g, _):
        def own_half(i, _):
            d = peer(i, 1 - side)
            take = pl.ds(pl.multiple_of(d * CHUNK + g * PIECE + ch * 8, 8), 8)
            give = pl.ds(pl.multiple_of(r * CHUNK + g * PIECE + ch * 8, 8), 8)
            remote(sent.at[take], arrived.at[give], send_sem.at[g], recv_sem.at[g], d, ch).start()
            return 0

        lax.fori_loop(0, PEERS // 2, own_half, 0)

        def block(l_hi, _):
            result = spread(rows_ref, facet_held[g * 2 + l_hi])
            for c in range(2):
                for e in range(2):
                    for d in range(0, 64, 8):
                        m = c * 128 + e * 64 + d
                        start = d * 32 + g * 8 + c * 4 + l_hi * 2 + e
                        facet_sent[pl.ds(start, 8, stride=32), :] = result[m : m + 8]
            return 0

        lax.fori_loop(0, 2, block, 0, unroll=True)

        def other_half(i, _):
            d = peer(i, 1 - side)
            take = pl.ds(pl.multiple_of(d * 32 + g * 8, 8), 8)
            give = pl.ds(pl.multiple_of(r * CHUNK + g * PIECE + ch * 8, 8), 8)
            remote(facet_sent.at[take], arrived.at[give], send_sem.at[g], recv_sem.at[g], d, other).start()
            return 0

        lax.fori_loop(0, PEERS // 2, other_half, 0)
        return 0

    lax.fori_loop(0, PIECES, facet_piece, 0)

    for load in loads[3:4] + loads[6:]:
        load.wait()
    sums[...] = jnp.zeros_like(sums)

    def column_piece(g, _):
        def block(i, _):
            l_hi, e = i // 2, i % 2
            rows = []
            for c in range(2):
                for jh in range(2):
                    rows.append(arrived[pl.ds(chunk_row(g, c, jh * 2 + l_hi, e), PEERS, stride=CHUNK), :])
            result = gather(jnp.concatenate(rows), columns_ref)
            for q_lo in range(8):
                row = pl.ds(pl.multiple_of(((e * 4 + g) * 8 + q_lo) * 32 + l_hi * 16, 16), 16)
                wide[0, row, :] = result[q_lo * 16 : q_lo * 16 + 16, 0:WIDE]
                wide[1, row, :] = result[q_lo * 16 : q_lo * 16 + 16, WIDE:]
            return 0

        lax.fori_loop(0, 4, block, 0, unroll=True)

        def short(e, _):
            q_hi = e * 4 + g
            items = []
            for l in range(RADIX):
                row = pl.ds(q_hi * 256 + l, 8, stride=32)
                items.append(
                    c_mul((wide[0, row, :], wide[1, row, :]), tw_ref[0, pl.ds(l, 1), :], tw_ref[1, pl.ds(l, 1), :])
                )
            freq = short_fft(items, -1)
            total, total_vis = sums[0], sums[1]
            items = []
            for v in range(RADIX):
                weight = weight_ref[q_hi, v]
                vis_re, vis_im = vis_ref[0, q_hi, v], vis_ref[1, q_hi, v]
                re = dual_ref[0, q_hi, v] * (1.0 / data_step) + weight * freq[v][0] - vis_re
                im = dual_ref[1, q_hi, v] * (1.0 / data_step) + weight * freq[v][1] - vis_im
                total = total + (re * re + im * im)
                total_vis = total_vis + (vis_re * vis_re + vis_im * vis_im)
                fourier_ref[0, q_hi, v] = re
                fourier_ref[1, q_hi, v] = im
                items.append((weight * re, weight * im))
            sums[0] = total
            sums[1] = total_vis
            done = short_fft(items, 1)
            for l in range(RADIX):
                re, im = c_mul(done[l], tw_ref[0, pl.ds(l, 1), :], -tw_ref[1, pl.ds(l, 1), :])
                row = pl.ds((l % 16) * 8, 8)
                held[(l // 16) * 8 + q_hi, row, 0:WIDE] = re
                held[(l // 16) * 8 + q_hi, row, WIDE:] = im
            return 0

        lax.fori_loop(0, 2, short, 0)

        def block_back(i, _):
            l_hi, e = i // 2, i % 2
            result = spread(columns_ref, held[l_hi * 8 + e * 4 + g])
            for c in range(2):
                for jh in range(2):
                    for s in range(0, 64, 8):
                        m = c * 128 + jh * 64 + s
                        start = s * CHUNK + chunk_row(g, c, jh * 2 + l_hi, e)
                        sent_back[pl.ds(start, 8, stride=CHUNK), :] = result[m : m + 8]
            return 0

        lax.fori_loop(0, 4, block_back, 0, unroll=True)
        back_copies(g, side, 1)
        mine = pl.ds(pl.multiple_of(r * CHUNK + g * PIECE, PIECE), PIECE)
        own = pltpu.make_async_copy(sent_back.at[mine], returned.at[mine], own_sem)
        own.start()
        own.wait()
        return 0

    def later_piece(g, _):
        all_of(sent, arrived, send_sem, recv_sem, g).wait_recv()
        column_piece(g, 0)
        back_copies(g - 1, 1 - side, 0)
        return 0

    lane = lax.broadcasted_iota(jnp.int32, (8, 128), 1)

    def filter_column(load, low_set, high_set, carry):
        taps = [load(p) for p in range(5)]
        low = taps[0] * low_set[0]
        high = taps[0] * high_set[0]
        for p in range(1, 5):
            low = low + taps[p] * low_set[p]
            high = high + taps[p] * high_set[p]
        return finish_column(low, high, low_set, high_set, carry)

    def finish_column(low, high, low_set, high_set, carry):
        old0, old1, unfinished = carry
        terms = [high * low_set[p] + low * high_set[p] for p in range(5)]
        new0 = pltpu.roll(terms[0], 2, 1)
        new1 = pltpu.roll(terms[1], 1, 1)
        new3 = pltpu.roll(terms[3], 127, 1)
        new4 = pltpu.roll(terms[4], 126, 1)
        finished = unfinished + jnp.where(lane >= 127, new3, 0.0) + jnp.where(lane >= 126, new4, 0.0)
        started = (
            terms[2]
            + (jnp.where(lane >= 2, new0, old0) + jnp.where(lane >= 1, new1, old1))
            + (jnp.where(lane < 127, new3, 0.0) + jnp.where(lane < 126, new4, 0.0))
        )
        return finished, (new0, new1, started)

    zero = jnp.zeros((8, 128), F32)
    prior_copies = [
        remote(wavelet_ref.at[other], prior_got, pri_send.at[0], pri_recv.at[0], r, other)
    ] + [
        remote(
            edge_send.at[c], edge_got.at[1 - ch], pri_send.at[1 + c], pri_recv.at[2 - ch],
            lax.rem(r + PEERS - 1 + 2 * ch, PEERS), c,
        )
        for c in range(2)
    ]

    def prior_step():
        for load in loads[4:6]:
            load.wait()
        for k in range(2):
            remote(far_send.at[0], far_got.at[k], sky_send.at[2], sky_recv.at[2 + k], r, other).wait_recv()
        no_far = jnp.logical_or(
            jnp.logical_and(ch == 0, r == 0), jnp.logical_and(ch == 1, r == PEERS - 1)
        )

        def grow(t, _):
            for k in range(4):
                grown[ch, t, 8 + 8 * k : 16 + 8 * k, :] = x_ref[ch * 4 + k, t]
                grown[other, t, 8 + 8 * k : 16 + 8 * k, :] = sky_got[k, t]
            near_own = jnp.where(first_here, x_ref[4, t][0:2], x_ref[3, t][6:8])
            near_other = near_got[t]
            far_own = jnp.where(no_far, 0.0, far_got[ch, t])
            far_other = jnp.where(no_far, 0.0, far_got[other, t])
            grown[ch, t, 6:8, :] = jnp.where(first_here, far_own, near_own)
            grown[ch, t, 40:42, :] = jnp.where(first_here, near_own, far_own)
            grown[other, t, 6:8, :] = jnp.where(first_here, far_other, near_other)
            grown[other, t, 40:42, :] = jnp.where(first_here, near_other, far_other)
            return 0

        lax.fori_loop(0, 32, grow, 0)

        def close(t, filtered):
            for k in range(4):
                s0 = prior_ref[0, k, t] + filtered[0][k]
                s1 = prior_ref[1, k, t] + filtered[1][k]
                limit = limit_ref[k, t]
                scale = limit / jnp.maximum(jnp.sqrt(s0 * s0 + s1 * s1), limit)
                wavelet_ref[0, k, t] = s0 * scale
                wavelet_ref[1, k, t] = s1 * scale

        def columns(t, carry):
            filtered, new = [[], []], []
            for c in range(2):
                for k in range(4):
                    finished, kept = filter_column(
                        lambda p: grown[c, t, 6 + 8 * k + p : 14 + 8 * k + p, :], low_taps, high_taps, carry[c * 4 + k]
                    )
                    filtered[c].append(finished)
                    new.append(kept)
            close(jnp.maximum(t - 1, 0), filtered)
            return tuple(new)

        carry = lax.fori_loop(0, 32, columns, ((zero, zero, zero),) * 8)
        close(31, [[carry[c * 4 + k][2] for k in range(4)] for c in range(2)])

        def edge(t, _):
            for c in range(2):
                edge_send[c, t] = jnp.where(
                    first_here, wavelet_ref[c, 0, t][0:2], wavelet_ref[c, 3, t][6:8]
                )
            return 0

        lax.fori_loop(0, 32, edge, 0)


    def adjoint_step():
        prior_copies[0].wait_recv()
        for k in range(2):
            remote(edge_send.at[0], edge_got.at[k], pri_send.at[1], pri_recv.at[1 + k], r, other).wait_recv()

        def fill(t, _):
            for k in range(4):
                mine = pl.ds(pl.multiple_of(8 + ch * 32 + 8 * k, 8), 8)
                theirs = pl.ds(pl.multiple_of(8 + other * 32 + 8 * k, 8), 8)
                spread_new[t, mine, :] = wavelet_ref[ch, k, t]
                spread_new[t, theirs, :] = prior_got[k, t]
            spread_new[t, 6:8, :] = jnp.where(r == 0, 0.0, edge_got[0, t])
            spread_new[t, 72:74, :] = jnp.where(r == PEERS - 1, 0.0, edge_got[1, t])
            return 0

        lax.fori_loop(0, 32, fill, 0)

        def close(t, k, filtered):
            image_ref[k, t] = x_ref[k, t] - primal_step * filtered

        def columns(t, carry):
            new = []
            for k in range(8):
                finished, kept = filter_column(
                    lambda p: spread_new[t, 6 + 8 * k + p : 14 + 8 * k + p, :], low_reverse, high_reverse, carry[k]
                )
                close(jnp.maximum(t - 1, 0), k, finished)
                new.append(kept)
            return tuple(new)

        carry = lax.fori_loop(0, 32, columns, ((zero, zero, zero),) * 8)
        for k in range(8):
            close(31, k, carry[k][2])

    prior_step()
    all_of(sent, arrived, send_sem, recv_sem, 0).wait_recv()
    for copy in prior_copies:
        copy.start()
    column_piece(0, 0)
    lax.fori_loop(1, PIECES, later_piece, 0)
    back_copies(PIECES - 1, 1 - side, 0)

    own_sums[0:1] = jnp.sum(sums[0], axis=0, keepdims=True)
    own_sums[1:2] = jnp.sum(sums[1], axis=0, keepdims=True)
    all_sums[r] = own_sums[...]

    def tell(i, _):
        remote(own_sums, all_sums.at[r], sum_send, sum_recv, lax.rem(r + i, PEERS), ch).start()
        return 0

    lax.fori_loop(1, PEERS, tell, 0)
    adjoint_step()
    every = pl.ds(0, PEERS - 1)
    told = remote(all_sums.at[every], all_sums.at[every], sum_send, sum_recv, after, ch)
    def back_piece(g, _):
        all_of(sent_back, returned, back_send, back_recv, g).wait_recv()

        def block(a_hi, _):
            rows = []
            for c in range(2):
                for e in range(2):
                    rows.append(returned[pl.ds(chunk_row(g, c, a_hi, e), PEERS, stride=CHUNK), :])
            result = gather(jnp.concatenate(rows), rows_ref)
            for a_lo in range(16):
                row = pl.ds(pl.multiple_of((a_hi * 16 + a_lo) * 32 + g * 8, 8), 8)
                wide[0, row, :] = result[a_lo * 8 : a_lo * 8 + 8, 0:WIDE]
                wide[1, row, :] = result[a_lo * 8 : a_lo * 8 + 8, WIDE:]
            return 0

        lax.fori_loop(0, 4, block, 0, unroll=True)
        return 0

    lax.fori_loop(0, PIECES, back_piece, 0)

    told.wait_recv()
    norms = jnp.sum(all_sums[...], axis=0)
    resid_norm = jnp.sum(norms[0:1], axis=1, keepdims=True)
    data_norm = jnp.sum(norms[1:2], axis=1, keepdims=True)
    shrink = data_step * (1.0 - radius_ref[0] * jnp.sqrt(data_norm) / jnp.sqrt(resid_norm))
    shrink = jnp.broadcast_to(shrink, (8, 128))
    factor_ref[...] = shrink * primal_step

    def scale(i, _):
        for v in range(32):
            for part in range(2):
                fourier_ref[part, i, v] = fourier_ref[part, i, v] * shrink
        return 0

    lax.fori_loop(0, 8, scale, 0)


    for copy in sky_copies + [far_up, far_down] + prior_copies + [told]:
        copy.wait_send()

    def drain(g, _):
        all_of(sent, arrived, send_sem, recv_sem, g).wait_send()
        all_of(sent_back, returned, back_send, back_recv, g).wait_send()
        return 0

    lax.fori_loop(0, PIECES, drain, 0)


def store(base, fourier, wavelet, wide, factor, tw_hbm, out_image, out_fourier, out_wavelet, image, tw_ref, sem, image_sem):
    table = pltpu.make_async_copy(tw_hbm, tw_ref, sem.at[2])
    table.start()
    copies = [
        pltpu.make_async_copy(src, dst, sem.at[i])
        for i, (src, dst) in enumerate(((fourier, out_fourier), (wavelet, out_wavelet)))
    ]
    for copy in copies:
        copy.start()
    table.wait()

    def image_copy(at):
        return pltpu.make_async_copy(image.at[at], out_image.at[at], image_sem.at[at])

    def finish(at, _):
        items = []
        for q in range(RADIX):
            row = pl.ds(at * 256 + q, 8, stride=32)
            items.append(
                c_mul((wide[0, row, :], wide[1, row, :]), tw_ref[0, pl.ds(q, 1), :], -tw_ref[1, pl.ds(q, 1), :])
            )
        done = short_fft(items, 1)
        for p in range(RADIX):
            image[at, p] = jnp.maximum(base[at, p] - done[p][0] * factor[...], 0.0)
        image_copy(at).start()
        return 0

    lax.fori_loop(0, 8, finish, 0)
    for copy in copies:
        copy.wait()
    for at in range(8):
        image_copy(at).wait()


def tiles(array):
    lead, n = array.shape[:-2], array.ndim - 2
    array = array.reshape(lead + (array.shape[-2] // 8, 8, 32, 128))
    return array.transpose(tuple(range(n)) + (n, n + 2, n + 1, n + 3))


def untiles(array):
    n = array.ndim - 4
    rows = array.shape[n] * 8
    array = array.transpose(tuple(range(n)) + (n, n + 2, n + 1, n + 3))
    return array.reshape(array.shape[:n] + (rows, SIDE))


def per_device(sky_image, fourier_dual, visibilities, weights, radius, wavelet_dual, reweight):
    forward, backward = dft_matrix(-1.0), dft_matrix(1.0)
    tables = (
        twiddle(-1.0),
        high_low(halves_first(backward))[0],
        high_low(halves_first(forward))[0],
    )
    vmem, dma = pltpu.VMEM, pltpu.SemaphoreType.DMA
    in_vmem, in_hbm = pl.BlockSpec(memory_space=pltpu.VMEM), pl.BlockSpec(memory_space=pltpu.HBM)
    results = pl.pallas_call(
        step,
        out_shape=(
            jax.ShapeDtypeStruct((8, 32, 8, 128), F32),
            jax.ShapeDtypeStruct((2, 8, 32, 8, 128), F32),
            jax.ShapeDtypeStruct((2, 4, 32, 8, 128), F32),
            jax.ShapeDtypeStruct((2, 2048, 128), F32),
            jax.ShapeDtypeStruct((8, 128), F32),
        ),
        in_specs=[pl.BlockSpec(memory_space=pltpu.SMEM)] + [in_hbm] * 9,
        out_specs=(in_vmem,) * 5,
        scratch_shapes=[
            vmem((8, 32, 8, 128), F32), vmem((2, 8, 32, 8, 128), F32), vmem((2, 8, 32, 8, 128), F32),
            vmem((8, 32, 8, 128), F32), vmem((2, 4, 32, 8, 128), F32), vmem((4, 32, 8, 128), F32),
            vmem((2, RADIX, WIDE), F32), vmem((2, 256, 256), jnp.bfloat16), vmem((2, 256, 256), jnp.bfloat16),
            vmem((4096, 128), F32), vmem((4096, 128), F32), vmem((4096, 128), F32), vmem((4096, 128), F32),
            vmem((16, 128, 256), F32), vmem((8, 128, 256), F32), vmem((2048, 128), F32),
            vmem((2, 8, 128), F32), vmem((2, 128), F32), vmem((PEERS, 2, 128), F32),
            vmem((32, 2, 128), F32), vmem((2, 32, 2, 128), F32),
            vmem((4, 32, 8, 128), F32), vmem((32, 2, 128), F32), vmem((2, 32, 2, 128), F32),
            vmem((2, 32, 48, 128), F32),
            vmem((2, 32, 2, 128), F32), vmem((4, 32, 8, 128), F32), vmem((2, 32, 2, 128), F32),
            vmem((32, 80, 128), F32),
            dma((9,)), dma, dma((PIECES,)), dma((PIECES,)), dma((PIECES,)), dma((PIECES,)),
            dma, dma, dma((4,)), dma((4,)), dma((3,)), dma((3,)),
        ],
        compiler_params=pltpu.CompilerParams(
            collective_id=0, has_side_effects=True, vmem_limit_bytes=VMEM_MIB << 20
        ),
    )(
        radius, *(pltpu.with_memory_space_constraint(v, pltpu.HBM) for v in (
            *map(tiles, (sky_image[0], wavelet_dual, reweight, fourier_dual[:, 0], visibilities[:, 0], weights[0])), *tables)),
    )
    image, fourier_new, wavelet_new = pl.pallas_call(
        store,
        out_shape=tuple(jax.ShapeDtypeStruct(v.shape, F32) for v in results[:3]),
        in_specs=[in_vmem] * 5 + [in_hbm],
        out_specs=(in_hbm,) * 3,
        scratch_shapes=[vmem((8, 32, 8, 128), F32), vmem((2, RADIX, WIDE), F32), dma((3,)), dma((8,))],
        compiler_params=pltpu.CompilerParams(vmem_limit_bytes=8 << 20),
    )(*results, pltpu.with_memory_space_constraint(tables[0], pltpu.HBM))
    return (untiles(image)[None], untiles(fourier_new)[:, None], untiles(wavelet_new))


def solution(mesh):
    in_specs = (
        P("chan", "row", None),
        P(None, "chan", "row", None),
        P(None, "chan", "row", None),
        P("chan", "row", None),
        P("chan"),
        P(None, ("row", "chan"), None),
        P(("row", "chan"), None),
    )
    out_specs = (
        P("chan", "row", None),
        P(None, "chan", "row", None),
        P(None, ("row", "chan"), None),
    )
    return jax.shard_map(
        per_device, mesh=mesh, in_specs=in_specs, out_specs=out_specs, check_vma=False
    )
```

```python
import math

import jax
import jax.numpy as jnp
import numpy as np
from jax import lax
from jax.experimental import pallas as pl
from jax.experimental.pallas import tpu as pltpu
from jax.sharding import PartitionSpec as P

data_step = 0.8
primal_step = 0.5
low_taps = (0.0625, 0.25, 0.375, 0.25, 0.0625)
high_taps = (-0.1, -0.3, 0.7, -0.2, -0.1)
low_reverse = (0.0625, 0.25, 0.375, 0.25, 0.0625)
high_reverse = (-0.1, -0.2, 0.7, -0.3, -0.1)

F32 = jnp.float32
SIDE = 4096
RADIX = 32
WIDE = 128


def c_add(a, b):
    re = a[0] + b[0]
    if a[1] is None:
        return (re, b[1])
    return (re, a[1] if b[1] is None else a[1] + b[1])


def c_sub(a, b):
    re = a[0] - b[0]
    if a[1] is None:
        return (re, None if b[1] is None else -b[1])
    return (re, a[1] if b[1] is None else a[1] - b[1])


def c_turn(a, k, n, orient):
    re, im = a
    if k == 0:
        return a
    if 4 * k == n:
        if im is None:
            return (None, re if orient > 0 else -re)
        return (-im, re) if orient > 0 else (im, -re)
    cos, sin = math.cos(2 * math.pi * k / n), orient * math.sin(2 * math.pi * k / n)
    if im is None:
        return (re * cos, re * sin)
    if 8 * k == n:
        return ((re - im) * cos, (re + im) * cos) if orient > 0 else ((re + im) * cos, (im - re) * cos)
    if 8 * k == 3 * n:
        c = -cos
        return ((-re - im) * c, (re - im) * c) if orient > 0 else ((im - re) * c, (-re - im) * c)
    return (re * cos - im * sin, re * sin + im * cos)


def short_fft(items, orient):
    n = len(items)
    if n == 1:
        return list(items)
    even = short_fft(items[0::2], orient)
    odd = short_fft(items[1::2], orient)
    low, high = [], []
    for k in range(n // 2):
        if even[k][1] is None and odd[k][1] is None and 4 * k == n:
            low.append((even[k][0], orient * odd[k][0]))
            high.append((even[k][0], -orient * odd[k][0]))
            continue
        turned = c_turn(odd[k], k, n, orient)
        low.append(c_add(even[k], turned))
        high.append(c_sub(even[k], turned))
    return low + high


def dft_matrix(orient):
    idx = np.arange(WIDE)
    angle = 2 * np.pi * ((idx[:, None] * idx[None, :]) % WIDE) / WIDE
    cos, sin = np.cos(angle) / 64.0, orient * np.sin(angle) / 64.0
    return np.block([[cos, sin], [-sin, cos]])


def halves_first(matrix_rows):
    order = np.arange(WIDE).reshape(64, 2).T.reshape(-1)
    return np.concatenate([matrix_rows[:WIDE][order], matrix_rows[WIDE:][order]])


def high_low(matrix):

    bf = np.asarray(matrix, np.float32).astype(jnp.bfloat16)
    low = (np.asarray(matrix) - bf.astype(np.float64)).astype(jnp.bfloat16)
    return (jnp.asarray(np.stack([bf, low])),)


def twiddle(orient):
    angle = 2 * np.pi * (np.arange(RADIX)[:, None] * np.arange(WIDE)[None, :]) / SIDE
    return jnp.asarray(np.stack([np.cos(angle), orient * np.sin(angle)]), jnp.float32)


def split_two(x):
    high = x.astype(jnp.bfloat16)
    return high, (x - high.astype(jnp.float32)).astype(jnp.bfloat16)


def product(dims, a_pair, b_pair):
    def one(a, b):
        return lax.dot_general(a, b, (dims, ((), ())), preferred_element_type=jnp.float32)

    return one(a_pair[0], b_pair[0]) + (one(a_pair[1], b_pair[0]) + one(a_pair[0], b_pair[1]))


def spread(matrix_ref, block):
    return product(((1,), (1,)), (matrix_ref[0], matrix_ref[1]), split_two(block))


def gather(block, matrix_ref):
    return product(((0,), (0,)), split_two(block), (matrix_ref[0], matrix_ref[1]))


def c_mul(a, b_re, b_im):
    return (a[0] * b_re - a[1] * b_im, a[0] * b_im + a[1] * b_re)


MESH = pl.DeviceIdType.MESH
PEERS = 64
CHUNK = 64
PIECE = 16
PIECES = 4
VMEM_MIB = 40


def chunk_row(g, c, a_hi, e):
    return g * PIECE + (a_hi // 2) * 8 + c * 4 + (a_hi % 2) * 2 + e


def step(
    radius_ref, x_hbm, prior_hbm, limit_hbm, dual_hbm, vis_hbm, weight_hbm, tw_hbm, rows_hbm, columns_hbm,
    image_ref, fourier_ref, wavelet_ref, wide, factor_ref,
    x_ref, dual_ref, vis_ref, weight_ref, prior_ref, limit_ref, tw_ref, rows_ref, columns_ref,
    sent, arrived, sent_back, returned, held, facet_held, facet_sent, sums, own_sums, all_sums,
    near_send, far_send, sky_got, near_got, far_got, grown, edge_send, prior_got, edge_got, spread_new,
    load_sem, own_sem, send_sem, recv_sem, back_send, back_recv, sum_send, sum_recv, sky_send, sky_recv, pri_send, pri_recv,
):
    r, ch = lax.axis_index("row"), lax.axis_index("chan")
    other = 1 - ch
    after, before = lax.rem(r + 1, PEERS), lax.rem(r + PEERS - 1, PEERS)

    side, z, low = (r // 8) % 2, r // 16, r % 8

    def peer(i, its_side):
        return lax.rem(z + i // 8, 4) * 16 + its_side * 8 + lax.rem(low + i % 8, 8)

    barrier = pltpu.get_barrier_semaphore()

    def greet(i, _):
        pl.semaphore_signal(barrier, inc=1, device_id=(lax.rem(r + i, PEERS), ch), device_id_type=MESH)
        return 0

    def greet_other(i, _):
        pl.semaphore_signal(barrier, inc=1, device_id=(peer(i, 1 - side), other), device_id_type=MESH)
        return 0

    lax.fori_loop(0, PEERS // 2, greet_other, 0)
    lax.fori_loop(1, PEERS, greet, 0)
    for row in (after, before, r):
        pl.semaphore_signal(barrier, inc=1, device_id=(row, other), device_id_type=MESH)

    loads = [
        pltpu.make_async_copy(src, dst, load_sem.at[i])
        for i, (src, dst) in enumerate(
            (
                (x_hbm, x_ref), (tw_hbm, tw_ref), (rows_hbm, rows_ref), (columns_hbm, columns_ref),
                (prior_hbm, prior_ref), (limit_hbm, limit_ref),
                (dual_hbm, dual_ref), (vis_hbm, vis_ref), (weight_hbm, weight_ref),
            )
        )
    ]
    for load in loads:
        load.start()

    def remote(src, dst, send, recv, row, chan):
        return pltpu.make_async_remote_copy(
            src_ref=src, dst_ref=dst, send_sem=send, recv_sem=recv, device_id=(row, chan), device_id_type=MESH
        )

    loads[0].wait()
    loads[1].wait()

    def turn_rows(done, into, blocks, at):
        a_hi, a_mid = at // 2, at % 2
        for q in range(RADIX):
            value = done[q]
            if value[1] is None:
                re = value[0] * tw_ref[0, pl.ds(q, 1), :]
                im = value[0] * tw_ref[1, pl.ds(q, 1), :]
            else:
                re, im = c_mul(value, tw_ref[0, pl.ds(q, 1), :], tw_ref[1, pl.ds(q, 1), :])
            row = pl.ds(pl.multiple_of((q % 8) * 16 + a_mid * 8, 8), 8)
            into[(q // 8) * blocks + a_hi, row, 0:WIDE] = re
            into[(q // 8) * blocks + a_hi, row, WIDE:] = im

    def row_short(at, _):
        items = [(x_ref[at, p], None) for p in range(RADIX)]
        done = short_fft(items, -1)
        turn_rows(done, held, 4, at)
        return 0

    lax.fori_loop(0, 8, row_short, 0)

    first_here = ch == 0

    def edges(t, _):
        low, high = x_ref[4, t][0:2], x_ref[3, t][6:8]
        near_send[t] = jnp.where(first_here, high, low)
        far_send[0, t] = x_ref[7, t][6:8]
        far_send[1, t] = x_ref[0, t][0:2]
        return 0

    lax.fori_loop(0, 32, edges, 0)
    pl.semaphore_wait(barrier, PEERS - 1 + PEERS // 2 + 3)

    half = pl.ds(pl.multiple_of(other * 4, 4), 4)
    sky_copies = [
        remote(x_ref.at[half], sky_got, sky_send.at[0], sky_recv.at[0], r, other),
        remote(near_send, near_got, sky_send.at[1], sky_recv.at[1], r, other),
    ]
    for copy in sky_copies:
        copy.start()
    far_up = remote(far_send.at[0], far_got.at[ch], sky_send.at[2], sky_recv.at[2 + ch], after, 0)
    far_down = remote(far_send.at[1], far_got.at[ch], sky_send.at[3], sky_recv.at[2 + ch], before, 1)
    far_up.start()
    far_down.start()

    loads[2].wait()
    def back_copies(g, its_side, first):
        def one(i, _):
            d = peer(i, its_side)
            take = pl.ds(pl.multiple_of(d * CHUNK + g * PIECE, PIECE), PIECE)
            give = pl.ds(pl.multiple_of(r * CHUNK + g * PIECE, PIECE), PIECE)
            remote(sent_back.at[take], returned.at[give], back_send.at[g], back_recv.at[g], d, ch).start()
            return 0

        lax.fori_loop(first, PEERS // 2, one, 0)

    def all_of(src, dst, send, recv, g):
        rows = pl.ds(0, (PEERS - 1) * PIECE)
        return remote(src.at[rows], dst.at[rows], send.at[g], recv.at[g], after, ch)

    def row_piece(g, _):
        def block(a_hi, _):
            result = spread(rows_ref, held[g * 4 + a_hi])
            for c in range(2):
                for e in range(2):
                    for d in range(0, 64, 8):
                        m = c * 128 + e * 64 + d
                        sent[pl.ds(d * CHUNK + chunk_row(g, c, a_hi, e), 8, stride=CHUNK), :] = result[m : m + 8]
            return 0

        lax.fori_loop(0, 4, block, 0, unroll=True)

        def one(i, _):
            d = peer(i, side)
            take = pl.ds(pl.multiple_of(d * CHUNK + g * PIECE, PIECE), PIECE)
            give = pl.ds(pl.multiple_of(r * CHUNK + g * PIECE, PIECE), PIECE)
            remote(sent.at[take], arrived.at[give], send_sem.at[g], recv_sem.at[g], d, ch).start()
            return 0

        lax.fori_loop(1, PEERS // 2, one, 0)
        mine = pl.ds(pl.multiple_of(r * CHUNK + g * PIECE, PIECE), PIECE)
        own = pltpu.make_async_copy(sent.at[mine], arrived.at[mine], own_sem)
        own.start()
        own.wait()
        return 0

    lax.fori_loop(0, PIECES, row_piece, 0)

    for copy in sky_copies:
        copy.wait_recv()

    def facet_short(at, _):
        done = short_fft([(sky_got[at, p], None) for p in range(RADIX)], -1)
        turn_rows(done, facet_held, 2, at)
        return 0

    lax.fori_loop(0, 4, facet_short, 0)

    def facet_piece(g, _):
        def own_half(i, _):
            d = peer(i, 1 - side)
            take = pl.ds(pl.multiple_of(d * CHUNK + g * PIECE + ch * 8, 8), 8)
            give = pl.ds(pl.multiple_of(r * CHUNK + g * PIECE + ch * 8, 8), 8)
            remote(sent.at[take], arrived.at[give], send_sem.at[g], recv_sem.at[g], d, ch).start()
            return 0

        lax.fori_loop(0, PEERS // 2, own_half, 0)

        def block(l_hi, _):
            result = spread(rows_ref, facet_held[g * 2 + l_hi])
            for c in range(2):
                for e in range(2):
                    for d in range(0, 64, 8):
                        m = c * 128 + e * 64 + d
                        start = d * 32 + g * 8 + c * 4 + l_hi * 2 + e
                        facet_sent[pl.ds(start, 8, stride=32), :] = result[m : m + 8]
            return 0

        lax.fori_loop(0, 2, block, 0, unroll=True)

        def other_half(i, _):
            d = peer(i, 1 - side)
            take = pl.ds(pl.multiple_of(d * 32 + g * 8, 8), 8)
            give = pl.ds(pl.multiple_of(r * CHUNK + g * PIECE + ch * 8, 8), 8)
            remote(facet_sent.at[take], arrived.at[give], send_sem.at[g], recv_sem.at[g], d, other).start()
            return 0

        lax.fori_loop(0, PEERS // 2, other_half, 0)
        return 0

    lax.fori_loop(0, PIECES, facet_piece, 0)

    for load in loads[3:4] + loads[6:]:
        load.wait()
    sums[...] = jnp.zeros_like(sums)

    def column_piece(g, _):
        def block(i, _):
            l_hi, e = i // 2, i % 2
            rows = []
            for c in range(2):
                for jh in range(2):
                    rows.append(arrived[pl.ds(chunk_row(g, c, jh * 2 + l_hi, e), PEERS, stride=CHUNK), :])
            result = gather(jnp.concatenate(rows), columns_ref)
            for q_lo in range(8):
                row = pl.ds(pl.multiple_of(((e * 4 + g) * 8 + q_lo) * 32 + l_hi * 16, 16), 16)
                wide[0, row, :] = result[q_lo * 16 : q_lo * 16 + 16, 0:WIDE]
                wide[1, row, :] = result[q_lo * 16 : q_lo * 16 + 16, WIDE:]
            return 0

        lax.fori_loop(0, 4, block, 0, unroll=True)

        def short(e, _):
            q_hi = e * 4 + g
            items = []
            for l in range(RADIX):
                row = pl.ds(q_hi * 256 + l, 8, stride=32)
                items.append(
                    c_mul((wide[0, row, :], wide[1, row, :]), tw_ref[0, pl.ds(l, 1), :], tw_ref[1, pl.ds(l, 1), :])
                )
            freq = short_fft(items, -1)
            total, total_vis = sums[0], sums[1]
            items = []
            for v in range(RADIX):
                weight = weight_ref[q_hi, v]
                vis_re, vis_im = vis_ref[0, q_hi, v], vis_ref[1, q_hi, v]
                re = dual_ref[0, q_hi, v] * (1.0 / data_step) + weight * freq[v][0] - vis_re
                im = dual_ref[1, q_hi, v] * (1.0 / data_step) + weight * freq[v][1] - vis_im
                total = total + (re * re + im * im)
                total_vis = total_vis + (vis_re * vis_re + vis_im * vis_im)
                fourier_ref[0, q_hi, v] = re
                fourier_ref[1, q_hi, v] = im
                items.append((weight * re, weight * im))
            sums[0] = total
            sums[1] = total_vis
            done = short_fft(items, 1)
            for l in range(RADIX):
                re, im = c_mul(done[l], tw_ref[0, pl.ds(l, 1), :], -tw_ref[1, pl.ds(l, 1), :])
                row = pl.ds((l % 16) * 8, 8)
                held[(l // 16) * 8 + q_hi, row, 0:WIDE] = re
                held[(l // 16) * 8 + q_hi, row, WIDE:] = im
            return 0

        lax.fori_loop(0, 2, short, 0)

        def block_back(i, _):
            l_hi, e = i // 2, i % 2
            result = spread(columns_ref, held[l_hi * 8 + e * 4 + g])
            for c in range(2):
                for jh in range(2):
                    for s in range(0, 64, 8):
                        m = c * 128 + jh * 64 + s
                        start = s * CHUNK + chunk_row(g, c, jh * 2 + l_hi, e)
                        sent_back[pl.ds(start, 8, stride=CHUNK), :] = result[m : m + 8]
            return 0

        lax.fori_loop(0, 4, block_back, 0, unroll=True)
        back_copies(g, side, 1)
        mine = pl.ds(pl.multiple_of(r * CHUNK + g * PIECE, PIECE), PIECE)
        own = pltpu.make_async_copy(sent_back.at[mine], returned.at[mine], own_sem)
        own.start()
        own.wait()
        return 0

    def later_piece(g, _):
        all_of(sent, arrived, send_sem, recv_sem, g).wait_recv()
        column_piece(g, 0)
        back_copies(g - 1, 1 - side, 0)
        return 0

    lane = lax.broadcasted_iota(jnp.int32, (8, 128), 1)

    def filter_column(load, low_set, high_set, carry):
        taps = [load(p) for p in range(5)]
        low = taps[0] * low_set[0]
        high = taps[0] * high_set[0]
        for p in range(1, 5):
            low = low + taps[p] * low_set[p]
            high = high + taps[p] * high_set[p]
        return finish_column(low, high, low_set, high_set, carry)

    def finish_column(low, high, low_set, high_set, carry):
        old0, old1, unfinished = carry
        terms = [high * low_set[p] + low * high_set[p] for p in range(5)]
        new0 = pltpu.roll(terms[0], 2, 1)
        new1 = pltpu.roll(terms[1], 1, 1)
        new3 = pltpu.roll(terms[3], 127, 1)
        new4 = pltpu.roll(terms[4], 126, 1)
        finished = unfinished + jnp.where(lane >= 127, new3, 0.0) + jnp.where(lane >= 126, new4, 0.0)
        started = (
            terms[2]
            + (jnp.where(lane >= 2, new0, old0) + jnp.where(lane >= 1, new1, old1))
            + (jnp.where(lane < 127, new3, 0.0) + jnp.where(lane < 126, new4, 0.0))
        )
        return finished, (new0, new1, started)

    zero = jnp.zeros((8, 128), F32)
    prior_copies = [
        remote(wavelet_ref.at[other], prior_got, pri_send.at[0], pri_recv.at[0], r, other)
    ] + [
        remote(
            edge_send.at[c], edge_got.at[1 - ch], pri_send.at[1 + c], pri_recv.at[2 - ch],
            lax.rem(r + PEERS - 1 + 2 * ch, PEERS), c,
        )
        for c in range(2)
    ] + [remote(edge_send.at[2], edge_got.at[2], pri_send.at[3], pri_recv.at[3], r, other)]

    def prior_step():
        for load in loads[4:6]:
            load.wait()
        for k in range(2):
            remote(far_send.at[0], far_got.at[k], sky_send.at[2], sky_recv.at[2 + k], r, other).wait_recv()
        no_far = jnp.logical_or(
            jnp.logical_and(ch == 0, r == 0), jnp.logical_and(ch == 1, r == PEERS - 1)
        )

        def grow(t, _):
            for k in range(4):
                grown[ch, t, 8 + 8 * k : 16 + 8 * k, :] = x_ref[ch * 4 + k, t]
                grown[other, t, 8 + 8 * k : 16 + 8 * k, :] = sky_got[k, t]
            near_own = jnp.where(first_here, x_ref[4, t][0:2], x_ref[3, t][6:8])
            near_other = near_got[t]
            far_own = jnp.where(no_far, 0.0, far_got[ch, t])
            far_other = jnp.where(no_far, 0.0, far_got[other, t])
            grown[ch, t, 6:8, :] = jnp.where(first_here, far_own, near_own)
            grown[ch, t, 40:42, :] = jnp.where(first_here, near_own, far_own)
            grown[other, t, 6:8, :] = jnp.where(first_here, far_other, near_other)
            grown[other, t, 40:42, :] = jnp.where(first_here, near_other, far_other)
            return 0

        lax.fori_loop(0, 32, grow, 0)

        def close(t, filtered):
            for k in range(4):
                s0 = prior_ref[0, k, t] + filtered[0][k]
                s1 = prior_ref[1, k, t] + filtered[1][k]
                limit = limit_ref[k, t]
                scale = limit / jnp.maximum(jnp.sqrt(s0 * s0 + s1 * s1), limit)
                wavelet_ref[0, k, t] = s0 * scale
                wavelet_ref[1, k, t] = s1 * scale

        def columns(t, carry):
            filtered, new = [[], []], []
            for c in range(2):
                for k in range(4):
                    finished, kept = filter_column(
                        lambda p: grown[c, t, 6 + 8 * k + p : 14 + 8 * k + p, :], low_taps, high_taps, carry[c * 4 + k]
                    )
                    filtered[c].append(finished)
                    new.append(kept)
            close(jnp.maximum(t - 1, 0), filtered)
            return tuple(new)

        carry = lax.fori_loop(0, 32, columns, ((zero, zero, zero),) * 8)
        close(31, [[carry[c * 4 + k][2] for k in range(4)] for c in range(2)])

        def edge(t, _):
            for c in range(2):
                edge_send[c, t] = jnp.where(
                    first_here, wavelet_ref[c, 0, t][0:2], wavelet_ref[c, 3, t][6:8]
                )
            edge_send[2, t] = jnp.where(first_here, wavelet_ref[other, 3, t][6:8], wavelet_ref[other, 0, t][0:2])
            return 0

        lax.fori_loop(0, 32, edge, 0)


    def adjoint_half(half, rows, near_above, near_below):
        def fill(t, _):
            for k in range(4):
                spread_new[half, t, 8 + 8 * k : 16 + 8 * k, :] = rows(k, t)
            above = jnp.where(r == 0, 0.0, edge_got[0, t])
            below = jnp.where(r == PEERS - 1, 0.0, edge_got[1, t])
            spread_new[half, t, 6:8, :] = jnp.where(half == 0, above, near_above(t))
            spread_new[half, t, 40:42, :] = jnp.where(half == 0, near_below(t), below)
            return 0

        lax.fori_loop(0, 32, fill, 0)

        def close(t, k, filtered):
            image_ref[half * 4 + k, t] = x_ref[half * 4 + k, t] - primal_step * filtered

        def columns(t, carry):
            new = []
            for k in range(4):
                finished, kept = filter_column(
                    lambda p: spread_new[half, t, 6 + 8 * k + p : 14 + 8 * k + p, :], low_reverse, high_reverse, carry[k]
                )
                close(jnp.maximum(t - 1, 0), k, finished)
                new.append(kept)
            return tuple(new)

        carry = lax.fori_loop(0, 32, columns, ((zero, zero, zero),) * 4)
        for k in range(4):
            close(31, k, carry[k][2])

    def adjoint_step():
        for k in range(3):
            remote(edge_send.at[0], edge_got.at[k], pri_send.at[1], pri_recv.at[1 + k], r, other).wait_recv()
        adjoint_half(ch, lambda k, t: wavelet_ref[ch, k, t], lambda t: edge_got[2, t], lambda t: edge_got[2, t])
        prior_copies[0].wait_recv()
        adjoint_half(
            other, lambda k, t: prior_got[k, t],
            lambda t: wavelet_ref[ch, 3, t][6:8], lambda t: wavelet_ref[ch, 0, t][0:2],
        )

    prior_step()
    all_of(sent, arrived, send_sem, recv_sem, 0).wait_recv()
    for copy in prior_copies[1:] + prior_copies[:1]:
        copy.start()
    column_piece(0, 0)
    lax.fori_loop(1, PIECES, later_piece, 0)
    back_copies(PIECES - 1, 1 - side, 0)

    own_sums[0:1] = jnp.sum(sums[0], axis=0, keepdims=True)
    own_sums[1:2] = jnp.sum(sums[1], axis=0, keepdims=True)
    all_sums[r] = own_sums[...]

    def tell(i, _):
        remote(own_sums, all_sums.at[r], sum_send, sum_recv, lax.rem(r + i, PEERS), ch).start()
        return 0

    lax.fori_loop(1, PEERS, tell, 0)
    adjoint_step()
    every = pl.ds(0, PEERS - 1)
    told = remote(all_sums.at[every], all_sums.at[every], sum_send, sum_recv, after, ch)
    def back_piece(g, _):
        all_of(sent_back, returned, back_send, back_recv, g).wait_recv()

        def block(a_hi, _):
            rows = []
            for c in range(2):
                for e in range(2):
                    rows.append(returned[pl.ds(chunk_row(g, c, a_hi, e), PEERS, stride=CHUNK), :])
            result = gather(jnp.concatenate(rows), rows_ref)
            for a_lo in range(16):
                row = pl.ds(pl.multiple_of((a_hi * 16 + a_lo) * 32 + g * 8, 8), 8)
                wide[0, row, :] = result[a_lo * 8 : a_lo * 8 + 8, 0:WIDE]
                wide[1, row, :] = result[a_lo * 8 : a_lo * 8 + 8, WIDE:]
            return 0

        lax.fori_loop(0, 4, block, 0, unroll=True)
        return 0

    lax.fori_loop(0, PIECES, back_piece, 0)

    told.wait_recv()
    norms = jnp.sum(all_sums[...], axis=0)
    resid_norm = jnp.sum(norms[0:1], axis=1, keepdims=True)
    data_norm = jnp.sum(norms[1:2], axis=1, keepdims=True)
    shrink = data_step * (1.0 - radius_ref[0] * jnp.sqrt(data_norm) / jnp.sqrt(resid_norm))
    shrink = jnp.broadcast_to(shrink, (8, 128))
    factor_ref[...] = shrink * primal_step

    def scale(i, _):
        for v in range(32):
            for part in range(2):
                fourier_ref[part, i, v] = fourier_ref[part, i, v] * shrink
        return 0

    lax.fori_loop(0, 8, scale, 0)


    for copy in sky_copies + [far_up, far_down] + prior_copies + [told]:
        copy.wait_send()

    def drain(g, _):
        all_of(sent, arrived, send_sem, recv_sem, g).wait_send()
        all_of(sent_back, returned, back_send, back_recv, g).wait_send()
        return 0

    lax.fori_loop(0, PIECES, drain, 0)


def store(base, fourier, wavelet, wide, factor, tw_hbm, out_image, out_fourier, out_wavelet, image, tw_ref, sem, image_sem):
    table = pltpu.make_async_copy(tw_hbm, tw_ref, sem.at[2])
    table.start()
    copies = [
        pltpu.make_async_copy(src, dst, sem.at[i])
        for i, (src, dst) in enumerate(((fourier, out_fourier), (wavelet, out_wavelet)))
    ]
    for copy in copies:
        copy.start()
    table.wait()

    def image_copy(at):
        return pltpu.make_async_copy(image.at[at], out_image.at[at], image_sem.at[at])

    def finish(at, _):
        items = []
        for q in range(RADIX):
            row = pl.ds(at * 256 + q, 8, stride=32)
            items.append(
                c_mul((wide[0, row, :], wide[1, row, :]), tw_ref[0, pl.ds(q, 1), :], -tw_ref[1, pl.ds(q, 1), :])
            )
        done = short_fft(items, 1)
        for p in range(RADIX):
            image[at, p] = jnp.maximum(base[at, p] - done[p][0] * factor[...], 0.0)
        image_copy(at).start()
        return 0

    lax.fori_loop(0, 8, finish, 0)
    for copy in copies:
        copy.wait()
    for at in range(8):
        image_copy(at).wait()


def tiles(array):
    lead, n = array.shape[:-2], array.ndim - 2
    array = array.reshape(lead + (array.shape[-2] // 8, 8, 32, 128))
    return array.transpose(tuple(range(n)) + (n, n + 2, n + 1, n + 3))


def untiles(array):
    n = array.ndim - 4
    rows = array.shape[n] * 8
    array = array.transpose(tuple(range(n)) + (n, n + 2, n + 1, n + 3))
    return array.reshape(array.shape[:n] + (rows, SIDE))


def per_device(sky_image, fourier_dual, visibilities, weights, radius, wavelet_dual, reweight):
    forward, backward = dft_matrix(-1.0), dft_matrix(1.0)
    tables = (
        twiddle(-1.0),
        high_low(halves_first(backward))[0],
        high_low(halves_first(forward))[0],
    )
    vmem, dma = pltpu.VMEM, pltpu.SemaphoreType.DMA
    in_vmem, in_hbm = pl.BlockSpec(memory_space=pltpu.VMEM), pl.BlockSpec(memory_space=pltpu.HBM)
    results = pl.pallas_call(
        step,
        out_shape=(
            jax.ShapeDtypeStruct((8, 32, 8, 128), F32),
            jax.ShapeDtypeStruct((2, 8, 32, 8, 128), F32),
            jax.ShapeDtypeStruct((2, 4, 32, 8, 128), F32),
            jax.ShapeDtypeStruct((2, 2048, 128), F32),
            jax.ShapeDtypeStruct((8, 128), F32),
        ),
        in_specs=[pl.BlockSpec(memory_space=pltpu.SMEM)] + [in_hbm] * 9,
        out_specs=(in_vmem,) * 5,
        scratch_shapes=[
            vmem((8, 32, 8, 128), F32), vmem((2, 8, 32, 8, 128), F32), vmem((2, 8, 32, 8, 128), F32),
            vmem((8, 32, 8, 128), F32), vmem((2, 4, 32, 8, 128), F32), vmem((4, 32, 8, 128), F32),
            vmem((2, RADIX, WIDE), F32), vmem((2, 256, 256), jnp.bfloat16), vmem((2, 256, 256), jnp.bfloat16),
            vmem((4096, 128), F32), vmem((4096, 128), F32), vmem((4096, 128), F32), vmem((4096, 128), F32),
            vmem((16, 128, 256), F32), vmem((8, 128, 256), F32), vmem((2048, 128), F32),
            vmem((2, 8, 128), F32), vmem((2, 128), F32), vmem((PEERS, 2, 128), F32),
            vmem((32, 2, 128), F32), vmem((2, 32, 2, 128), F32),
            vmem((4, 32, 8, 128), F32), vmem((32, 2, 128), F32), vmem((2, 32, 2, 128), F32),
            vmem((2, 32, 48, 128), F32),
            vmem((3, 32, 2, 128), F32), vmem((4, 32, 8, 128), F32), vmem((3, 32, 2, 128), F32),
            vmem((2, 32, 48, 128), F32),
            dma((9,)), dma, dma((PIECES,)), dma((PIECES,)), dma((PIECES,)), dma((PIECES,)),
            dma, dma, dma((4,)), dma((4,)), dma((4,)), dma((4,)),
        ],
        compiler_params=pltpu.CompilerParams(
            collective_id=0, has_side_effects=True, vmem_limit_bytes=VMEM_MIB << 20
        ),
    )(
        radius, *(pltpu.with_memory_space_constraint(v, pltpu.HBM) for v in (
            *map(tiles, (sky_image[0], wavelet_dual, reweight, fourier_dual[:, 0], visibilities[:, 0], weights[0])), *tables)),
    )
    image, fourier_new, wavelet_new = pl.pallas_call(
        store,
        out_shape=tuple(jax.ShapeDtypeStruct(v.shape, F32) for v in results[:3]),
        in_specs=[in_vmem] * 5 + [in_hbm],
        out_specs=(in_hbm,) * 3,
        scratch_shapes=[vmem((8, 32, 8, 128), F32), vmem((2, RADIX, WIDE), F32), dma((3,)), dma((8,))],
        compiler_params=pltpu.CompilerParams(vmem_limit_bytes=8 << 20),
    )(*results, pltpu.with_memory_space_constraint(tables[0], pltpu.HBM))
    return (untiles(image)[None], untiles(fourier_new)[:, None], untiles(wavelet_new))


def solution(mesh):
    in_specs = (
        P("chan", "row", None),
        P(None, "chan", "row", None),
        P(None, "chan", "row", None),
        P("chan", "row", None),
        P("chan"),
        P(None, ("row", "chan"), None),
        P(("row", "chan"), None),
    )
    out_specs = (
        P("chan", "row", None),
        P(None, "chan", "row", None),
        P(None, ("row", "chan"), None),
    )
    return jax.shard_map(
        per_device, mesh=mesh, in_specs=in_specs, out_specs=out_specs, check_vma=False
    )
```
